256 devices in a mesh: gx: 8 (over z_lo, y), gy: 8 (over z_hi, core), gz: 4 (over x).
Axes of the slice: x: 4, y: 4, z: 8 (z_hi: 4, z_lo: 2; z = z_hi * 2 + z_lo), core: 2. Of those that a mesh axis runs over, the one named last changes fastest.
Arguments:
- e_adjoint: float32 [3, 256, 128, 1024], P(None, 'gx', 'gy', 'gz'), may hold values from -6 to 6
- h_adjoint: float32 [3, 256, 128, 1024], P(None, 'gx', 'gy', 'gz'), may hold values from -6 to 6
- snapshots: bfloat16 [3, 3, 256, 128, 1024], P(None, None, 'gx', 'gy', 'gz'), may hold values from -6 to 6
- material: int32 [256, 128, 1024], P('gx', 'gy', 'gz'), may hold values from 0 to 7
- permittivity: float32 [8], replicated, may hold values from 1 to 12
- design_mask: int32 [256, 128], P('gx', 'gy'), may hold values from 0 to 1
- ports: int32 [3], replicated, may hold values from 0 to 33554431
- amplitudes: float32 [2, 3], replicated, may hold values from -8 to 8
Outputs:
- e_final: float32 [3, 256, 128, 1024], P(None, 'gx', 'gy', 'gz')
- h_final: float32 [3, 256, 128, 1024], P(None, 'gx', 'gy', 'gz')
- gradient: float32 [256, 128], P('gx', ('gy', 'gz'))
The draws below stay inside these ranges and needn't reach their ends.
All inputs are finite; a program needn't handle non-finite values.
Results may differ from the reference program's by a relative error of at most 0.0003.
Values sent between devices are 32-bit elements; how exact they have to be, the bound alone decides.
A program may use at most 64 MiB of HBM per device.

```python
import math
import jax
import jax.numpy as jnp
from jax import lax

NMAT = 8
NPORT = 3
STEPS = 2
NX = 256
NY = 128
NZ = 1024


def with_ends(result, key, least, high):
    place = [jax.random.randint(jax.random.fold_in(key, axis), (), 0, length) for axis, length in enumerate(result.shape)]
    widest = result.shape.index(max(result.shape))
    beside = place[:widest] + [(place[widest] + 1) % result.shape[widest]] + place[widest + 1:]
    return result.at[tuple(place)].set(least).at[tuple(beside)].set(high)


def block_scale(own_key, extent, cuts, smallest, largest):
    gain, own = 1.0, jax.random.fold_in(own_key, 6)
    for axis_at, blocks in cuts:
        steps = jnp.exp(jax.random.uniform(jax.random.fold_in(own, axis_at), (blocks,), jnp.float32, smallest / len(cuts), largest / len(cuts)))
        gain = gain * jnp.repeat(steps, extent[axis_at] // blocks).reshape([-1 if axis == axis_at else 1 for axis in range(len(extent))])
    return gain


def scatter_about(own_key, extent, deviation, most, split=(), held_as=jnp.bfloat16):
    loudness = block_scale(own_key, extent, split, -0.22, 0.18) if split else 1.0
    values = jax.random.normal(own_key, extent, jnp.float32) * deviation * loudness
    return jnp.minimum(jnp.maximum(values, -most), most).astype(held_as)


def setup_inputs(seed: int = 0) -> dict:
    splits = jax.random.split(jax.random.key(seed), 9)
    return {
        "e_adjoint": scatter_about(splits[0], (3, NX, NY, NZ), 1.0, 6.0, ((1, 8), (2, 8), (3, 4)), jnp.float32),
        "h_adjoint": scatter_about(splits[1], (3, NX, NY, NZ), 1.0, 6.0, ((1, 8), (2, 8), (3, 4)), jnp.float32),
        "snapshots": scatter_about(splits[2], (STEPS + 1, 3, NX, NY, NZ), 1.0, 6.0, ((2, 8), (3, 8), (4, 4))),
        "material": with_ends(jax.random.randint(splits[3], (NX, NY, NZ), 0, NMAT), jax.random.fold_in(splits[3], 1), 0, NMAT - 1).astype(jnp.int32),
        "permittivity": jnp.clip(jnp.exp(jax.random.uniform(splits[4], (NMAT,), jnp.float32, math.log(1.0), math.log(12.0))), 1.0, 12.0),
        "design_mask": with_ends(jax.random.randint(splits[5], (NX, NY), 0, 2), jax.random.fold_in(splits[5], 1), 0, 1).astype(jnp.int32),
        "ports": jax.random.randint(splits[6], (NPORT,), 0, NX * NY * NZ).astype(jnp.int32),
        "amplitudes": scatter_about(splits[7], (STEPS, NPORT), 2.0, 8.0, (), jnp.float32),
    }


magnetic_step = 0.5
electric_step = 0.5


def shifted_up(field, axis):
    widths = [(0, 0), (0, 0), (0, 0)]
    widths[axis] = (0, 1)
    return jnp.pad(lax.slice_in_dim(field, 1, field.shape[axis], axis=axis), widths)


def shifted_down(field, axis):
    widths = [(0, 0), (0, 0), (0, 0)]
    widths[axis] = (1, 0)
    return jnp.pad(lax.slice_in_dim(field, 0, field.shape[axis] - 1, axis=axis), widths)


def curl_electric(field):
    comp_x, comp_y, comp_z = field[0], field[1], field[2]
    out_x = (shifted_up(comp_z, 1) - comp_z) - (shifted_up(comp_y, 2) - comp_y)
    out_y = (shifted_up(comp_x, 2) - comp_x) - (shifted_up(comp_z, 0) - comp_z)
    out_z = (shifted_up(comp_y, 0) - comp_y) - (shifted_up(comp_x, 1) - comp_x)
    return jnp.stack([out_x, out_y, out_z])


def curl_magnetic(field):
    comp_x, comp_y, comp_z = field[0], field[1], field[2]
    out_x = (comp_z - shifted_down(comp_z, 1)) - (comp_y - shifted_down(comp_y, 2))
    out_y = (comp_x - shifted_down(comp_x, 2)) - (comp_z - shifted_down(comp_z, 0))
    out_z = (comp_y - shifted_down(comp_y, 0)) - (comp_x - shifted_down(comp_x, 1))
    return jnp.stack([out_x, out_y, out_z])


def reference(e_adjoint, h_adjoint, snapshots, material, permittivity, design_mask, ports, amplitudes):
    coef = (electric_step / permittivity)[material]
    plane = NY * NZ
    port_x = (ports // plane).astype(jnp.int32)
    port_y = ((ports // NZ) % NY).astype(jnp.int32)
    port_z = (ports % NZ).astype(jnp.int32)
    electric = e_adjoint
    magnetic = h_adjoint
    corr = jnp.zeros(material.shape, jnp.float32)
    for step_no in range(STEPS):
        magnetic = magnetic - magnetic_step * curl_electric(electric)
        electric = electric + coef[None] * curl_magnetic(magnetic)
        electric = electric.at[2, port_x, port_y, port_z].add(amplitudes[step_no])
        change = snapshots[step_no].astype(jnp.float32) - snapshots[step_no + 1].astype(jnp.float32)
        corr = corr + jnp.sum(electric * change, axis=0)
    gradient = design_mask.astype(jnp.float32) * jnp.sum(corr, axis=2)
    return electric, magnetic, gradient
```

```python
import jax
import jax.numpy as jnp
from jax import lax
from jax.experimental import pallas as pl
from jax.experimental.pallas import tpu as pltpu
from jax.sharding import PartitionSpec as P

STEPS = 2
AXES = ("gx", "gy", "gz")
LANES = 128
ROWS = 8
half = 0.5

EX, EY, EZ, PX, PY, PZ, D1, D2, D3, D4, D5, D6 = range(12)
OFFSETS = (
    (-1, 0, 0), (0, -1, 0), (0, 0, -1),
    (1, 0, 0), (0, 1, 0), (0, 0, 1),
    (1, 0, -1), (1, -1, 0), (-1, 1, 0), (0, 1, -1), (0, -1, 1), (-1, 0, 1),
)


def kernel(mesh_sizes, extent, perm, ports, amps, e_in, h_in, s_in, m_in,
           e_out, h_out, g_out,
           e_v, h_v, s_v, m_v, c_v, corr_v, src_v,
           y_e, z_e, y_p, z_p, y_h, x_h, g_v,
           r_ex, r_ey, r_ez, r_px, r_py, r_pz, r_d1, r_d2, r_d3, r_d4, r_d5, r_d6, r_g,
           in_sem, out_sem, send_sem, recv_sem, gs_sem, gr_sem):
    _, lx, ly, lz = e_in.shape
    nmat = perm.shape[0]
    nport = ports.shape[0]
    me = tuple(lax.axis_index(a) for a in AXES)
    start = (me[0] * lx, me[1] * ly, me[2] * lz)
    nz_dev = mesh_sizes[2]

    def exists(off):
        ok = None
        for a in range(3):
            if off[a] == 0:
                continue
            c = me[a] + off[a]
            t = (c >= 0) & (c < mesh_sizes[a])
            ok = t if ok is None else ok & t
        return ok

    def at(off):
        return tuple(me[a] + off[a] for a in range(3))

    loads = [
        pltpu.make_async_copy(e_in, e_v, in_sem.at[0]),
        pltpu.make_async_copy(h_in, h_v, in_sem.at[1]),
        pltpu.make_async_copy(m_in, m_v, in_sem.at[2]),
        pltpu.make_async_copy(s_in, s_v, in_sem.at[3]),
    ]
    for c in loads:
        c.start()

    barrier = pltpu.get_barrier_semaphore()
    count = jnp.int32(0)
    greet = list(OFFSETS)
    for d in range(2, nz_dev):
        greet += [(0, 0, d), (0, 0, -d)]
    for off in greet:
        ok = exists(off)
        count = count + ok.astype(jnp.int32)

        @pl.when(ok)
        def _(off=off):
            pl.semaphore_signal(barrier, inc=1, device_id=at(off), device_id_type=pl.DeviceIdType.MESH)

    recv = (r_ex, r_ey, r_ez, r_px, r_py, r_pz, r_d1, r_d2, r_d3, r_d4, r_d5, r_d6)

    def source(msg, phase):
        e = e_in if phase == 0 else e_v
        if msg == EX:
            return e.at[1:3, 0]
        if msg == EY:
            return y_e.at[phase]
        if msg == EZ:
            return z_e.at[phase]
        if msg == PX:
            return h_v.at[1:3, lx - 1]
        if msg == PY:
            return y_p.at[phase]
        if msg == PZ:
            return z_p.at[phase]
        if msg == D1:
            return e.at[0, lx - 1, :, 0:LANES]
        if msg == D2:
            return e.at[0, lx - 1, 0:ROWS, :]
        if msg == D3:
            return e.at[1, 0, ly - ROWS:ly, :]
        if msg == D4:
            return z_e.at[phase, ly - ROWS:ly, :]
        if msg == D5:
            return z_e.at[phase, 0:ROWS, :]
        return e.at[2, 0, :, lz - LANES:lz]

    def copy(msg, phase):
        return pltpu.make_async_remote_copy(
            src_ref=source(msg, phase), dst_ref=recv[msg].at[phase],
            send_sem=send_sem.at[phase, msg], recv_sem=recv_sem.at[phase, msg],
            device_id=at(OFFSETS[msg]), device_id_type=pl.DeviceIdType.MESH)

    def send(msg, phase):
        @pl.when(exists(OFFSETS[msg]))
        def _():
            copy(msg, phase).start()

    def wait_send(msg, phase):
        @pl.when(exists(OFFSETS[msg]))
        def _():
            copy(msg, phase).wait_send()

    def comes(msg):
        return exists(tuple(-o for o in OFFSETS[msg]))

    def wait_recv(msg, phase):
        @pl.when(comes(msg))
        def _():
            copy(msg, phase).wait_recv()

    for msg in range(12):
        @pl.when(jnp.logical_not(comes(msg)))
        def _(msg=msg):
            recv[msg][...] = jnp.zeros(recv[msg].shape, jnp.float32)

    row = lax.broadcasted_iota(jnp.int32, (ly, lz), 0)
    lane = lax.broadcasted_iota(jnp.int32, (ly, lz), 1)
    row1 = lax.broadcasted_iota(jnp.int32, (ly, LANES), 0)
    lane1 = lax.broadcasted_iota(jnp.int32, (ly, LANES), 1)

    def zup(v):
        return jnp.where(lane == lz - 1, 0.0, pltpu.roll(v, lz - 1, 1))

    def yup(v):
        return jnp.where(row == ly - 1, 0.0, pltpu.roll(v, ly - 1, 0))

    def pick(tile, from_lane, x, slot, acc):
        to = slot * lx + x
        shift = lax.rem(to + (LANES - from_lane), LANES)
        return jnp.where(lane1 == to, pltpu.roll(tile, shift, 1), acc)

    def place(packed, to_lane, x, slot):
        shift = lax.rem(2 * LANES + to_lane - (slot * lx + x), LANES)
        return pltpu.roll(packed, shift, 1)

    pl.semaphore_wait(barrier, count)
    for msg in (EX, D1, D2, D3, D6):
        send(msg, 0)

    plane = extent[1] * extent[2]
    port_x = []
    for p in range(nport):
        cell = ports[p]
        px = lax.div(cell, plane)
        rest = lax.rem(cell, plane)
        py = lax.div(rest, extent[2]) - start[1]
        pz = lax.rem(rest, extent[2]) - start[2]
        port_x.append(px - start[0])
        hit = (row == py) & (lane == pz)
        for s in range(STEPS):
            src_v[s, p] = jnp.where(hit, amps[s, p], 0.0)
    for s in range(STEPS):
        src_v[s, nport] = jnp.zeros((ly, lz), jnp.float32)

    loads[0].wait()

    def pack_e(x, ex, ey, ez, phase, acc):
        y_e[phase, 0, pl.ds(x, 1), :] = ex[0:1, :]
        y_e[phase, 1, pl.ds(x, 1), :] = ez[0:1, :]
        acc = pick(ex[:, 0:LANES], 0, x, 0, acc)
        acc = pick(ey[:, 0:LANES], 0, x, 1, acc)
        return pick(ez[:, lz - LANES:lz], LANES - 1, x, 2, acc)

    zero1 = jnp.zeros((ly, LANES), jnp.float32)

    def first_pack(x, acc):
        return pack_e(x, e_v[0, x], e_v[1, x], e_v[2, x], 0, acc)

    z_e[0] = lax.fori_loop(0, lx, first_pack, zero1)
    for msg in (EY, EZ, D4, D5):
        send(msg, 0)
    loads[1].wait()

    def magnetic(phase):
        def one(x, acc, last):
            ex, ey, ez = e_v[0, x], e_v[1, x], e_v[2, x]
            if last:
                dey, dez = -ey, -ez
            else:
                dey, dez = e_v[1, x + 1] - ey, e_v[2, x + 1] - ez
            hx = h_v[0, x] - half * ((yup(ez) - ez) - (zup(ey) - ey))
            hy = h_v[1, x] - half * ((zup(ex) - ex) - dez)
            hz = h_v[2, x] - half * (dey - (yup(ex) - ex))
            h_v[0, x] = hx
            h_v[1, x] = hy
            h_v[2, x] = hz
            y_p[phase, 0, pl.ds(x, 1), :] = hx[ly - 1:ly, :]
            y_p[phase, 1, pl.ds(x, 1), :] = hz[ly - 1:ly, :]
            acc = pick(hx[:, lz - LANES:lz], LANES - 1, x, 0, acc)
            return pick(hy[:, lz - LANES:lz], LANES - 1, x, 1, acc)

        acc = lax.fori_loop(0, lx - 1, lambda x, a: one(x, a, False), zero1)
        z_p[phase] = one(lx - 1, acc, True)

    flags = tuple((me[a] > 0).astype(jnp.float32) for a in range(3))

    def halos(phase):
        fx, fy, fz = flags
        d1 = pltpu.roll(r_d1[phase], LANES - 1, 1)
        d1 = jnp.concatenate([jnp.zeros((ly, lz - LANES), jnp.float32), d1], 1) if lz > LANES else d1
        x_h[0] = (r_px[phase, 0] + half * e_v[2, 0]) * fx - jnp.where(lane == lz - 1, half * d1, 0.0)
        d2 = jnp.broadcast_to(r_d2[phase, 0:1, :], (ly, lz))
        x_h[1] = (r_px[phase, 1] - half * e_v[1, 0]) * fx + jnp.where(row == ly - 1, half * d2, 0.0)
        d4 = jnp.broadcast_to(r_d4[phase, ROWS - 1:ROWS, :], (lx, LANES))
        rx = lax.broadcasted_iota(jnp.int32, (lx, LANES), 0)
        cx = lax.broadcasted_iota(jnp.int32, (lx, LANES), 1)
        d4 = jnp.sum(jnp.where(cx == rx + lx, d4, 0.0), axis=1, keepdims=True)
        ry = lax.broadcasted_iota(jnp.int32, (lx, lz), 0)
        cy = lax.broadcasted_iota(jnp.int32, (lx, lz), 1)
        y_h[0] = (r_py[phase, 0] - half * y_e[phase, 1]) * fy + jnp.where(cy == lz - 1, half * d4, 0.0)
        d3 = jnp.broadcast_to(r_d3[phase, ROWS - 1:ROWS, :], (lx, lz))
        y_h[1] = (r_py[phase, 1] + half * y_e[phase, 0]) * fy - jnp.where(ry == lx - 1, half * d3, 0.0)
        own = z_e[phase]
        fix = jnp.where(lane1 < lx, half * pltpu.roll(own, LANES - lx, 1), -half * pltpu.roll(own, lx, 1))
        zh = (r_pz[phase] + fix) * fz
        d5 = jnp.broadcast_to(pltpu.roll(r_d5[phase], LANES - 2 * lx, 1)[0:1, :], (ly, LANES))
        zh = zh - jnp.where((row1 == ly - 1) & (lane1 < lx), half * d5, 0.0)
        d6 = pltpu.roll(r_d6[phase], 2 * lx, 1)
        zh = zh + jnp.where(lane1 == 2 * lx - 1, half * d6, 0.0)
        h_v[1, lx - 1] = h_v[1, lx - 1] + half * r_ex[phase, 1]
        h_v[2, lx - 1] = h_v[2, lx - 1] - half * r_ex[phase, 0]
        return zh

    def pad_high(t):
        return jnp.concatenate([jnp.zeros((ly, lz - LANES), jnp.float32), t], 1) if lz > LANES else t

    def pad_low(t):
        return jnp.concatenate([t, jnp.zeros((ly, lz - LANES), jnp.float32)], 1) if lz > LANES else t

    def electric(step, zh):
        phase = step
        ze = r_ez[phase]

        def one(x, carry):
            hy_b, hz_b, acc = carry
            ex, ey, ez = e_v[0, x], e_v[1, x], e_v[2, x]
            top_row = row == ly - 1
            top_lane = lane == lz - 1
            eyz = pad_high(place(ze, LANES - 1, x, 1))
            exz = pad_high(place(ze, LANES - 1, x, 0))
            exy = jnp.broadcast_to(r_ey[phase, 0, pl.ds(x, 1), :], (ly, lz))
            ezy = jnp.broadcast_to(r_ey[phase, 1, pl.ds(x, 1), :], (ly, lz))
            hx = h_v[0, x] - jnp.where(top_row, half * ezy, 0.0) + jnp.where(top_lane, half * eyz, 0.0)
            hy = h_v[1, x] - jnp.where(top_lane, half * exz, 0.0)
            hz = h_v[2, x] + jnp.where(top_row, half * exy, 0.0)
            h_v[0, x] = hx
            h_v[1, x] = hy
            h_v[2, x] = hz
            low_row = row == 0
            low_lane = lane == 0
            hx_y = jnp.where(low_row, jnp.broadcast_to(y_h[0, pl.ds(x, 1), :], (ly, lz)), pltpu.roll(hx, 1, 0))
            hz_y = jnp.where(low_row, jnp.broadcast_to(y_h[1, pl.ds(x, 1), :], (ly, lz)), pltpu.roll(hz, 1, 0))
            hx_z = jnp.where(low_lane, pad_low(place(zh, 0, x, 0)), pltpu.roll(hx, 1, 1))
            hy_z = jnp.where(low_lane, pad_low(place(zh, 0, x, 1)), pltpu.roll(hy, 1, 1))
            c = c_v[x]
            ex = ex + c * ((hz - hz_y) - (hy - hy_z))
            ey = ey + c * ((hx - hx_z) - (hz - hz_b))
            ez = ez + c * ((hy - hy_b) - (hx - hx_y))
            for p in range(nport):
                ez = ez + src_v[step, jnp.where(port_x[p] == x, p, nport)]
            e_v[0, x] = ex
            e_v[1, x] = ey
            e_v[2, x] = ez
            total = None
            for comp, val in enumerate((ex, ey, ez)):
                change = s_v[step, comp, x].astype(jnp.float32) - s_v[step + 1, comp, x].astype(jnp.float32)
                t = val * change
                total = t if total is None else total + t
            fold = total[:, 0:LANES]
            for k in range(1, lz // LANES):
                fold = fold + total[:, k * LANES:(k + 1) * LANES]
            if step == 0:
                corr_v[x] = fold
            else:
                fold = fold + corr_v[x]
            if step + 1 < STEPS:
                acc = pack_e(x, ex, ey, ez, phase + 1, acc)
            else:
                acc = jnp.where(lane1 == x, jnp.sum(fold, axis=1, keepdims=True), acc)
            return hy, hz, acc

        _, _, acc = lax.fori_loop(0, lx, one, (x_h[0], x_h[1], zero1))
        return acc

    magnetic(0)
    for msg in (PX, PY, PZ):
        send(msg, 0)

    loads[2].wait()
    coefs = [half / jnp.full((ly, lz), perm[k], jnp.float32) for k in range(nmat)]

    def coef_plane(x, carry):
        mat = m_v[x]
        c = coefs[0]
        for k in range(1, nmat):
            c = jnp.where(mat == k, coefs[k], c)
        c_v[x] = c
        return carry

    lax.fori_loop(0, lx, coef_plane, 0)
    loads[3].wait()

    for step in range(STEPS):
        if step > 0:
            for msg in (EX, D1, D2, D3, D6, EY, EZ, D4, D5):
                send(msg, step)
            magnetic(step)
            for msg in (PX, PY, PZ):
                send(msg, step)
        for msg in range(12):
            wait_send(msg, step)
        for msg in range(12):
            wait_recv(msg, step)
        zh = halos(step)
        acc = electric(step, zh)
        if step + 1 < STEPS:
            z_e[step + 1] = acc

    outs = [
        pltpu.make_async_copy(e_v, e_out, out_sem.at[0]),
        pltpu.make_async_copy(h_v, h_out, out_sem.at[1]),
    ]
    for c in outs:
        c.start()

    own_rows = ly // nz_dev
    g_v[...] = acc

    def tile_of(k):
        return pl.ds(pl.multiple_of((k * own_rows) // ROWS * ROWS, ROWS), ROWS)

    gcopies = []
    for d in range(1, nz_dev):
        peer = lax.rem(me[2] + d, nz_dev)
        gcopies.append(pltpu.make_async_remote_copy(
            src_ref=g_v.at[tile_of(peer)], dst_ref=r_g.at[d - 1],
            send_sem=gs_sem.at[d - 1], recv_sem=gr_sem.at[d - 1],
            device_id=(me[0], me[1], peer), device_id_type=pl.DeviceIdType.MESH))
    for c in gcopies:
        c.start()
    total = g_v[tile_of(me[2])]
    for d, c in enumerate(gcopies):
        c.wait_recv()
        total = total + r_g[d]
    shift = lax.rem(ROWS - lax.rem(me[2] * own_rows, ROWS), ROWS)
    g_out[...] = pltpu.roll(total, shift, 0)
    for c in gcopies:
        c.wait_send()
    for c in outs:
        c.wait()


def solution(mesh):
    mesh_sizes = tuple(mesh.shape[a] for a in AXES)

    def body(e_adjoint, h_adjoint, snapshots, material, permittivity, design_mask, ports, amplitudes):
        _, lx, ly, lz = e_adjoint.shape
        extent = (lx * mesh_sizes[0], ly * mesh_sizes[1], lz * mesh_sizes[2])
        nport = ports.shape[0]
        f32 = jnp.float32
        any_spec = pl.BlockSpec(memory_space=pl.ANY)
        smem = pl.BlockSpec(memory_space=pltpu.SMEM)
        e, h, g = pl.pallas_call(
            lambda *refs: kernel(mesh_sizes, extent, *refs),
            out_shape=(
                jax.ShapeDtypeStruct(e_adjoint.shape, f32),
                jax.ShapeDtypeStruct(h_adjoint.shape, f32),
                jax.ShapeDtypeStruct((ROWS, LANES), f32),
            ),
            in_specs=[smem, smem, smem, any_spec, any_spec, any_spec, any_spec],
            out_specs=(any_spec, any_spec, pl.BlockSpec(memory_space=pltpu.VMEM)),
            scratch_shapes=[
                pltpu.VMEM((3, lx, ly, lz), f32),
                pltpu.VMEM((3, lx, ly, lz), f32),
                pltpu.VMEM(snapshots.shape, snapshots.dtype),
                pltpu.VMEM((lx, ly, lz), jnp.int32),
                pltpu.VMEM((lx, ly, lz), f32),
                pltpu.VMEM((lx, ly, LANES), f32),
                pltpu.VMEM((STEPS, nport + 1, ly, lz), f32),
                pltpu.VMEM((STEPS, 2, lx, lz), f32),
                pltpu.VMEM((STEPS, ly, LANES), f32),
                pltpu.VMEM((STEPS, 2, lx, lz), f32),
                pltpu.VMEM((STEPS, ly, LANES), f32),
                pltpu.VMEM((2, lx, lz), f32),
                pltpu.VMEM((2, ly, lz), f32),
                pltpu.VMEM((ly, LANES), f32),
                pltpu.VMEM((STEPS, 2, ly, lz), f32),
                pltpu.VMEM((STEPS, 2, lx, lz), f32),
                pltpu.VMEM((STEPS, ly, LANES), f32),
                pltpu.VMEM((STEPS, 2, ly, lz), f32),
                pltpu.VMEM((STEPS, 2, lx, lz), f32),
                pltpu.VMEM((STEPS, ly, LANES), f32),
                pltpu.VMEM((STEPS, ly, LANES), f32),
                pltpu.VMEM((STEPS, ROWS, lz), f32),
                pltpu.VMEM((STEPS, ROWS, lz), f32),
                pltpu.VMEM((STEPS, ROWS, LANES), f32),
                pltpu.VMEM((STEPS, ROWS, LANES), f32),
                pltpu.VMEM((STEPS, ly, LANES), f32),
                pltpu.VMEM((3, ROWS, LANES), f32),
                pltpu.SemaphoreType.DMA((4,)),
                pltpu.SemaphoreType.DMA((2,)),
                pltpu.SemaphoreType.DMA((STEPS, 12)),
                pltpu.SemaphoreType.DMA((STEPS, 12)),
                pltpu.SemaphoreType.DMA((3,)),
                pltpu.SemaphoreType.DMA((3,)),
            ],
            compiler_params=pltpu.CompilerParams(collective_id=0, has_side_effects=True),
            name="reverse_steps",
        )(permittivity, ports, amplitudes, e_adjoint, h_adjoint, snapshots, material)
        own = ly // mesh_sizes[2]
        mask = lax.dynamic_slice_in_dim(design_mask, lax.axis_index("gz") * own, own, 1)
        gradient = mask.astype(f32) * g[:own, :lx].T
        return e, h, gradient

    placed = (
        P(None, "gx", "gy", "gz"),
        P(None, "gx", "gy", "gz"),
        P(None, None, "gx", "gy", "gz"),
        P("gx", "gy", "gz"),
        P(),
        P("gx", "gy"),
        P(),
        P(),
    )
    return jax.shard_map(
        body,
        mesh=mesh,
        in_specs=placed,
        out_specs=(P(None, "gx", "gy", "gz"), P(None, "gx", "gy", "gz"), P("gx", ("gy", "gz"))),
        check_vma=False,
    )
```

```python
import jax
import jax.numpy as jnp
from jax import lax
from jax.experimental import pallas as pl
from jax.experimental.pallas import tpu as pltpu
from jax.sharding import PartitionSpec as P

STEPS = 2
AXES = ("gx", "gy", "gz")
LANES = 128
ROWS = 8
half = 0.5
UP, UM, UE = 8, 8, 8

EX, EY, EZ, PX, PY, PZ, D1, D2, D3, D4, D5, D6 = range(12)
OFFSETS = (
    (-1, 0, 0), (0, -1, 0), (0, 0, -1),
    (1, 0, 0), (0, 1, 0), (0, 0, 1),
    (1, 0, -1), (1, -1, 0), (-1, 1, 0), (0, 1, -1), (0, -1, 1), (-1, 0, 1),
)


def kernel(mesh_sizes, extent, perm, ports, amps, e_in, h_in, s_in, m_in,
           e_out, h_out, g_out,
           e_v, h_v, s_v, m_v, c_v, corr_v, src_v,
           y_e, z_e, y_p, z_p, y_h, x_h, g_v,
           r_ex, r_ey, r_ez, r_px, r_py, r_pz, r_d1, r_d2, r_d3, r_d4, r_d5, r_d6, r_g,
           in_sem, out_sem, send_sem, recv_sem, gs_sem, gr_sem):
    _, lx, ly, lz = e_in.shape
    nmat = perm.shape[0]
    nport = ports.shape[0]
    me = tuple(lax.axis_index(a) for a in AXES)
    start = (me[0] * lx, me[1] * ly, me[2] * lz)
    nz_dev = mesh_sizes[2]

    def exists(off):
        ok = None
        for a in range(3):
            if off[a] == 0:
                continue
            c = me[a] + off[a]
            t = (c >= 0) & (c < mesh_sizes[a])
            ok = t if ok is None else ok & t
        return ok

    def at(off):
        return tuple(me[a] + off[a] for a in range(3))

    loads = [
        pltpu.make_async_copy(e_in, e_v.at[:, 0:lx], in_sem.at[0]),
        pltpu.make_async_copy(h_in, h_v, in_sem.at[1]),
        pltpu.make_async_copy(m_in, m_v, in_sem.at[2]),
        pltpu.make_async_copy(s_in, s_v, in_sem.at[3]),
    ]
    for c in loads:
        c.start()

    barrier = pltpu.get_barrier_semaphore()
    count = jnp.int32(0)
    greet = list(OFFSETS)
    for d in range(2, nz_dev):
        greet += [(0, 0, d), (0, 0, -d)]
    for off in greet:
        ok = exists(off)
        count = count + ok.astype(jnp.int32)

        @pl.when(ok)
        def _(off=off):
            pl.semaphore_signal(barrier, inc=1, device_id=at(off), device_id_type=pl.DeviceIdType.MESH)

    recv = (r_ex, r_ey, r_ez, r_px, r_py, r_pz, r_d1, r_d2, r_d3, r_d4, r_d5, r_d6)

    def source(msg, phase):
        e = e_in if phase == 0 else e_v
        if msg == EX:
            return e.at[1:3, 0]
        if msg == EY:
            return y_e.at[phase]
        if msg == EZ:
            return z_e.at[phase]
        if msg == PX:
            return h_v.at[1:3, lx - 1]
        if msg == PY:
            return y_p.at[phase]
        if msg == PZ:
            return z_p.at[phase]
        if msg == D1:
            return e.at[0, lx - 1, :, 0:LANES]
        if msg == D2:
            return e.at[0, lx - 1, 0:ROWS, :]
        if msg == D3:
            return e.at[1, 0, ly - ROWS:ly, :]
        if msg == D4:
            return z_e.at[phase, ly - ROWS:ly, :]
        if msg == D5:
            return z_e.at[phase, 0:ROWS, :]
        return e.at[2, 0, :, lz - LANES:lz]

    def copy(msg, phase):
        return pltpu.make_async_remote_copy(
            src_ref=source(msg, phase), dst_ref=recv[msg].at[phase],
            send_sem=send_sem.at[phase, msg], recv_sem=recv_sem.at[phase, msg],
            device_id=at(OFFSETS[msg]), device_id_type=pl.DeviceIdType.MESH)

    def send(msg, phase):
        @pl.when(exists(OFFSETS[msg]))
        def _():
            copy(msg, phase).start()

    def wait_send(msg, phase):
        @pl.when(exists(OFFSETS[msg]))
        def _():
            copy(msg, phase).wait_send()

    def comes(msg):
        return exists(tuple(-o for o in OFFSETS[msg]))

    def wait_recv(msg, phase):
        @pl.when(comes(msg))
        def _():
            copy(msg, phase).wait_recv()

    for c in (1, 2):
        e_v[c, lx] = jnp.zeros((ly, lz), jnp.float32)

    for msg in range(12):
        @pl.when(jnp.logical_not(comes(msg)))
        def _(msg=msg):
            recv[msg][...] = jnp.zeros(recv[msg].shape, jnp.float32)

    row = lax.broadcasted_iota(jnp.int32, (ly, lz), 0)
    lane = lax.broadcasted_iota(jnp.int32, (ly, lz), 1)
    row1 = lax.broadcasted_iota(jnp.int32, (ly, LANES), 0)
    lane1 = lax.broadcasted_iota(jnp.int32, (ly, LANES), 1)

    def zup(v):
        return jnp.where(lane == lz - 1, 0.0, pltpu.roll(v, lz - 1, 1))

    def yup(v):
        return jnp.where(row == ly - 1, 0.0, pltpu.roll(v, ly - 1, 0))

    def pick(tile, from_lane, x, slot, acc):
        to = slot * lx + x
        shift = lax.rem(to + (LANES - from_lane), LANES)
        return jnp.where(lane1 == to, pltpu.roll(tile, shift, 1), acc)

    def place(packed, to_lane, x, slot):
        shift = lax.rem(2 * LANES + to_lane - (slot * lx + x), LANES)
        return pltpu.roll(packed, shift, 1)

    pl.semaphore_wait(barrier, count)
    for msg in (EX, D1, D2, D3, D6):
        send(msg, 0)

    plane = extent[1] * extent[2]
    port_x = []
    for p in range(nport):
        cell = ports[p]
        px = lax.div(cell, plane)
        rest = lax.rem(cell, plane)
        py = lax.div(rest, extent[2]) - start[1]
        pz = lax.rem(rest, extent[2]) - start[2]
        port_x.append(px - start[0])
        hit = (row == py) & (lane == pz)
        for s in range(STEPS):
            src_v[s, p] = jnp.where(hit, amps[s, p], 0.0)
    for s in range(STEPS):
        src_v[s, nport] = jnp.zeros((ly, lz), jnp.float32)

    loads[0].wait()

    def pack_e(x, ex, ey, ez, phase, acc):
        y_e[phase, 0, pl.ds(x, 1), :] = ex[0:1, :]
        y_e[phase, 1, pl.ds(x, 1), :] = ez[0:1, :]
        acc = pick(ex[:, 0:LANES], 0, x, 0, acc)
        acc = pick(ey[:, 0:LANES], 0, x, 1, acc)
        return pick(ez[:, lz - LANES:lz], LANES - 1, x, 2, acc)

    zero1 = jnp.zeros((ly, LANES), jnp.float32)

    def first_pack(x, acc):
        return pack_e(x, e_v[0, x], e_v[1, x], e_v[2, x], 0, acc)

    z_e[0] = lax.fori_loop(0, lx, first_pack, zero1, unroll=UP)
    for msg in (EY, EZ, D4, D5):
        send(msg, 0)
    loads[1].wait()

    def magnetic(phase):
        def one(x, acc):
            ex, ey, ez = e_v[0, x], e_v[1, x], e_v[2, x]
            dey, dez = e_v[1, x + 1] - ey, e_v[2, x + 1] - ez
            hx = h_v[0, x] - half * ((yup(ez) - ez) - (zup(ey) - ey))
            hy = h_v[1, x] - half * ((zup(ex) - ex) - dez)
            hz = h_v[2, x] - half * (dey - (yup(ex) - ex))
            h_v[0, x] = hx
            h_v[1, x] = hy
            h_v[2, x] = hz
            y_p[phase, 0, pl.ds(x, 1), :] = hx[ly - 1:ly, :]
            y_p[phase, 1, pl.ds(x, 1), :] = hz[ly - 1:ly, :]
            acc = pick(hx[:, lz - LANES:lz], LANES - 1, x, 0, acc)
            return pick(hy[:, lz - LANES:lz], LANES - 1, x, 1, acc)

        z_p[phase] = lax.fori_loop(0, lx, one, zero1, unroll=UM)

    flags = tuple((me[a] > 0).astype(jnp.float32) for a in range(3))

    def halos(phase):
        fx, fy, fz = flags
        d1 = pltpu.roll(r_d1[phase], LANES - 1, 1)
        d1 = jnp.concatenate([jnp.zeros((ly, lz - LANES), jnp.float32), d1], 1) if lz > LANES else d1
        x_h[0] = (r_px[phase, 0] + half * e_v[2, 0]) * fx - jnp.where(lane == lz - 1, half * d1, 0.0)
        d2 = jnp.broadcast_to(r_d2[phase, 0:1, :], (ly, lz))
        x_h[1] = (r_px[phase, 1] - half * e_v[1, 0]) * fx + jnp.where(row == ly - 1, half * d2, 0.0)
        d4 = jnp.broadcast_to(r_d4[phase, ROWS - 1:ROWS, :], (lx, LANES))
        rx = lax.broadcasted_iota(jnp.int32, (lx, LANES), 0)
        cx = lax.broadcasted_iota(jnp.int32, (lx, LANES), 1)
        d4 = jnp.sum(jnp.where(cx == rx + lx, d4, 0.0), axis=1, keepdims=True)
        ry = lax.broadcasted_iota(jnp.int32, (lx, lz), 0)
        cy = lax.broadcasted_iota(jnp.int32, (lx, lz), 1)
        y_h[0] = (r_py[phase, 0] - half * y_e[phase, 1]) * fy + jnp.where(cy == lz - 1, half * d4, 0.0)
        d3 = jnp.broadcast_to(r_d3[phase, ROWS - 1:ROWS, :], (lx, lz))
        y_h[1] = (r_py[phase, 1] + half * y_e[phase, 0]) * fy - jnp.where(ry == lx - 1, half * d3, 0.0)
        own = z_e[phase]
        fix = jnp.where(lane1 < lx, half * pltpu.roll(own, LANES - lx, 1), -half * pltpu.roll(own, lx, 1))
        zh = (r_pz[phase] + fix) * fz
        d5 = jnp.broadcast_to(pltpu.roll(r_d5[phase], LANES - 2 * lx, 1)[0:1, :], (ly, LANES))
        zh = zh - jnp.where((row1 == ly - 1) & (lane1 < lx), half * d5, 0.0)
        d6 = pltpu.roll(r_d6[phase], 2 * lx, 1)
        zh = zh + jnp.where(lane1 == 2 * lx - 1, half * d6, 0.0)
        h_v[1, lx - 1] = h_v[1, lx - 1] + half * r_ex[phase, 1]
        h_v[2, lx - 1] = h_v[2, lx - 1] - half * r_ex[phase, 0]
        return zh

    def pad_high(t):
        return jnp.concatenate([jnp.zeros((ly, lz - LANES), jnp.float32), t], 1) if lz > LANES else t

    def pad_low(t):
        return jnp.concatenate([t, jnp.zeros((ly, lz - LANES), jnp.float32)], 1) if lz > LANES else t

    def electric(step, zh):
        phase = step
        ze = r_ez[phase]

        def one(x, carry):
            hy_b, hz_b, acc = carry
            ex, ey, ez = e_v[0, x], e_v[1, x], e_v[2, x]
            top_row = row == ly - 1
            top_lane = lane == lz - 1
            eyz = pad_high(place(ze, LANES - 1, x, 1))
            exz = pad_high(place(ze, LANES - 1, x, 0))
            exy = jnp.broadcast_to(r_ey[phase, 0, pl.ds(x, 1), :], (ly, lz))
            ezy = jnp.broadcast_to(r_ey[phase, 1, pl.ds(x, 1), :], (ly, lz))
            hx = h_v[0, x] - jnp.where(top_row, half * ezy, 0.0) + jnp.where(top_lane, half * eyz, 0.0)
            hy = h_v[1, x] - jnp.where(top_lane, half * exz, 0.0)
            hz = h_v[2, x] + jnp.where(top_row, half * exy, 0.0)
            h_v[0, x] = hx
            h_v[1, x] = hy
            h_v[2, x] = hz
            low_row = row == 0
            low_lane = lane == 0
            hx_y = jnp.where(low_row, jnp.broadcast_to(y_h[0, pl.ds(x, 1), :], (ly, lz)), pltpu.roll(hx, 1, 0))
            hz_y = jnp.where(low_row, jnp.broadcast_to(y_h[1, pl.ds(x, 1), :], (ly, lz)), pltpu.roll(hz, 1, 0))
            hx_z = jnp.where(low_lane, pad_low(place(zh, 0, x, 0)), pltpu.roll(hx, 1, 1))
            hy_z = jnp.where(low_lane, pad_low(place(zh, 0, x, 1)), pltpu.roll(hy, 1, 1))
            c = c_v[x]
            ex = ex + c * ((hz - hz_y) - (hy - hy_z))
            ey = ey + c * ((hx - hx_z) - (hz - hz_b))
            ez = ez + c * ((hy - hy_b) - (hx - hx_y))
            for p in range(nport):
                ez = ez + src_v[step, jnp.where(port_x[p] == x, p, nport)]
            e_v[0, x] = ex
            e_v[1, x] = ey
            e_v[2, x] = ez
            total = None
            for comp, val in enumerate((ex, ey, ez)):
                change = s_v[step, comp, x].astype(jnp.float32) - s_v[step + 1, comp, x].astype(jnp.float32)
                t = val * change
                total = t if total is None else total + t
            fold = total[:, 0:LANES]
            for k in range(1, lz // LANES):
                fold = fold + total[:, k * LANES:(k + 1) * LANES]
            if step == 0:
                corr_v[x] = fold
            else:
                fold = fold + corr_v[x]
            if step + 1 < STEPS:
                acc = pack_e(x, ex, ey, ez, phase + 1, acc)
            else:
                acc = jnp.where(lane1 == x, jnp.sum(fold, axis=1, keepdims=True), acc)
            return hy, hz, acc

        _, _, acc = lax.fori_loop(0, lx, one, (x_h[0], x_h[1], zero1), unroll=UE)
        return acc

    magnetic(0)
    for msg in (PX, PY, PZ):
        send(msg, 0)

    loads[2].wait()
    coefs = [half / jnp.full((ly, lz), perm[k], jnp.float32) for k in range(nmat)]

    def coef_plane(x, carry):
        mat = m_v[x]
        c = coefs[0]
        for k in range(1, nmat):
            c = jnp.where(mat == k, coefs[k], c)
        c_v[x] = c
        return carry

    lax.fori_loop(0, lx, coef_plane, 0, unroll=UP)
    loads[3].wait()

    for step in range(STEPS):
        if step > 0:
            for msg in (EX, D1, D2, D3, D6, EY, EZ, D4, D5):
                send(msg, step)
            magnetic(step)
            for msg in (PX, PY, PZ):
                send(msg, step)
        for msg in range(12):
            wait_send(msg, step)
        for msg in range(12):
            wait_recv(msg, step)
        zh = halos(step)
        acc = electric(step, zh)
        if step + 1 < STEPS:
            z_e[step + 1] = acc

    outs = [
        pltpu.make_async_copy(e_v.at[:, 0:lx], e_out, out_sem.at[0]),
        pltpu.make_async_copy(h_v, h_out, out_sem.at[1]),
    ]
    for c in outs:
        c.start()

    own_rows = ly // nz_dev
    tile = g_out.shape[0]
    g_v[...] = acc

    def tile_of(k):
        return pl.ds(pl.multiple_of((k * own_rows) // tile * tile, ROWS), tile)

    gcopies = []
    for d in range(1, nz_dev):
        peer = lax.rem(me[2] + d, nz_dev)
        gcopies.append(pltpu.make_async_remote_copy(
            src_ref=g_v.at[tile_of(peer)], dst_ref=r_g.at[d - 1],
            send_sem=gs_sem.at[d - 1], recv_sem=gr_sem.at[d - 1],
            device_id=(me[0], me[1], peer), device_id_type=pl.DeviceIdType.MESH))
    for c in gcopies:
        c.start()
    total = g_v[tile_of(me[2])]
    for d, c in enumerate(gcopies):
        c.wait_recv()
        total = total + r_g[d]
    shift = lax.rem(tile - lax.rem(me[2] * own_rows, tile), tile)
    g_out[...] = pltpu.roll(total, shift, 0)
    for c in gcopies:
        c.wait_send()
    for c in outs:
        c.wait()


def solution(mesh):
    mesh_sizes = tuple(mesh.shape[a] for a in AXES)

    def body(e_adjoint, h_adjoint, snapshots, material, permittivity, design_mask, ports, amplitudes):
        _, lx, ly, lz = e_adjoint.shape
        extent = (lx * mesh_sizes[0], ly * mesh_sizes[1], lz * mesh_sizes[2])
        nport = ports.shape[0]
        f32 = jnp.float32
        own = ly // mesh_sizes[2]
        tile = max(ROWS, own)
        any_spec = pl.BlockSpec(memory_space=pl.ANY)
        smem = pl.BlockSpec(memory_space=pltpu.SMEM)
        e, h, g = pl.pallas_call(
            lambda *refs: kernel(mesh_sizes, extent, *refs),
            out_shape=(
                jax.ShapeDtypeStruct(e_adjoint.shape, f32),
                jax.ShapeDtypeStruct(h_adjoint.shape, f32),
                jax.ShapeDtypeStruct((tile, LANES), f32),
            ),
            in_specs=[smem, smem, smem, any_spec, any_spec, any_spec, any_spec],
            out_specs=(any_spec, any_spec, pl.BlockSpec(memory_space=pltpu.VMEM)),
            scratch_shapes=[
                pltpu.VMEM((3, lx + 1, ly, lz), f32),
                pltpu.VMEM((3, lx, ly, lz), f32),
                pltpu.VMEM(snapshots.shape, snapshots.dtype),
                pltpu.VMEM((lx, ly, lz), jnp.int32),
                pltpu.VMEM((lx, ly, lz), f32),
                pltpu.VMEM((lx, ly, LANES), f32),
                pltpu.VMEM((STEPS, nport + 1, ly, lz), f32),
                pltpu.VMEM((STEPS, 2, lx, lz), f32),
                pltpu.VMEM((STEPS, ly, LANES), f32),
                pltpu.VMEM((STEPS, 2, lx, lz), f32),
                pltpu.VMEM((STEPS, ly, LANES), f32),
                pltpu.VMEM((2, lx, lz), f32),
                pltpu.VMEM((2, ly, lz), f32),
                pltpu.VMEM((ly, LANES), f32),
                pltpu.VMEM((STEPS, 2, ly, lz), f32),
                pltpu.VMEM((STEPS, 2, lx, lz), f32),
                pltpu.VMEM((STEPS, ly, LANES), f32),
                pltpu.VMEM((STEPS, 2, ly, lz), f32),
                pltpu.VMEM((STEPS, 2, lx, lz), f32),
                pltpu.VMEM((STEPS, ly, LANES), f32),
                pltpu.VMEM((STEPS, ly, LANES), f32),
                pltpu.VMEM((STEPS, ROWS, lz), f32),
                pltpu.VMEM((STEPS, ROWS, lz), f32),
                pltpu.VMEM((STEPS, ROWS, LANES), f32),
                pltpu.VMEM((STEPS, ROWS, LANES), f32),
                pltpu.VMEM((STEPS, ly, LANES), f32),
                pltpu.VMEM((3, tile, LANES), f32),
                pltpu.SemaphoreType.DMA((4,)),
                pltpu.SemaphoreType.DMA((2,)),
                pltpu.SemaphoreType.DMA((STEPS, 12)),
                pltpu.SemaphoreType.DMA((STEPS, 12)),
                pltpu.SemaphoreType.DMA((3,)),
                pltpu.SemaphoreType.DMA((3,)),
            ],
            compiler_params=pltpu.CompilerParams(collective_id=0, has_side_effects=True),
            name="reverse_steps",
        )(permittivity, ports, amplitudes, e_adjoint, h_adjoint, snapshots, material)
        mask = lax.dynamic_slice_in_dim(design_mask, lax.axis_index("gz") * own, own, 1)
        gradient = mask.astype(f32) * g[:own, :lx].T
        return e, h, gradient

    placed = (
        P(None, "gx", "gy", "gz"),
        P(None, "gx", "gy", "gz"),
        P(None, None, "gx", "gy", "gz"),
        P("gx", "gy", "gz"),
        P(),
        P("gx", "gy"),
        P(),
        P(),
    )
    return jax.shard_map(
        body,
        mesh=mesh,
        in_specs=placed,
        out_specs=(P(None, "gx", "gy", "gz"), P(None, "gx", "gy", "gz"), P("gx", ("gy", "gz"))),
        check_vma=False,
    )
```

```python
import jax
import jax.numpy as jnp
from jax import lax
from jax.experimental import pallas as pl
from jax.experimental.pallas import tpu as pltpu
from jax.sharding import PartitionSpec as P

STEPS = 2
AXES = ("gx", "gy", "gz")
LANES = 128
ROWS = 8
half = 0.5
UP, UM, UE = 8, 8, 8

EX, EY, EZ, PX, PY, PZ, D1, D2, D3, D4, D5, D6 = range(12)
OFFSETS = (
    (-1, 0, 0), (0, -1, 0), (0, 0, -1),
    (1, 0, 0), (0, 1, 0), (0, 0, 1),
    (1, 0, -1), (1, -1, 0), (-1, 1, 0), (0, 1, -1), (0, -1, 1), (-1, 0, 1),
)


def kernel(mesh_sizes, extent, perm, ports, amps, mask, e_in, h_in, s_in, m_in,
           e_v, h_v, g_out,
           s_v, m_v, c_v, corr_v, src_v,
           y_e, z_e, y_p, z_p, y_h, x_h, g_v,
           r_ex, r_ey, r_ez, r_px, r_py, r_pz, r_d1, r_d2, r_d3, r_d4, r_d5, r_d6, r_g,
           in_sem, send_sem, recv_sem, gs_sem, gr_sem):
    _, lx, ly, lz = e_in.shape
    nmat = perm.shape[0]
    nport = ports.shape[0]
    me = tuple(lax.axis_index(a) for a in AXES)
    start = (me[0] * lx, me[1] * ly, me[2] * lz)
    nz_dev = mesh_sizes[2]

    def exists(off):
        ok = None
        for a in range(3):
            if off[a] == 0:
                continue
            c = me[a] + off[a]
            t = (c >= 0) & (c < mesh_sizes[a])
            ok = t if ok is None else ok & t
        return ok

    def at(off):
        return tuple(me[a] + off[a] for a in range(3))

    loads = [
        pltpu.make_async_copy(e_in, e_v.at[:, 0:lx], in_sem.at[0]),
        pltpu.make_async_copy(h_in, h_v, in_sem.at[1]),
        pltpu.make_async_copy(m_in, m_v, in_sem.at[2]),
        pltpu.make_async_copy(s_in, s_v, in_sem.at[3]),
    ]
    for c in loads:
        c.start()

    barrier = pltpu.get_barrier_semaphore()
    count = jnp.int32(0)
    greet = list(OFFSETS)
    for d in range(2, nz_dev):
        greet += [(0, 0, d), (0, 0, -d)]
    for off in greet:
        ok = exists(off)
        count = count + ok.astype(jnp.int32)

        @pl.when(ok)
        def _(off=off):
            pl.semaphore_signal(barrier, inc=1, device_id=at(off), device_id_type=pl.DeviceIdType.MESH)

    recv = (r_ex, r_ey, r_ez, r_px, r_py, r_pz, r_d1, r_d2, r_d3, r_d4, r_d5, r_d6)

    def source(msg, phase):
        e = e_in if phase == 0 else e_v
        if msg == EX:
            return e.at[1:3, 0]
        if msg == EY:
            return y_e.at[phase]
        if msg == EZ:
            return z_e.at[phase]
        if msg == PX:
            return h_v.at[1:3, lx - 1]
        if msg == PY:
            return y_p.at[phase]
        if msg == PZ:
            return z_p.at[phase]
        if msg == D1:
            return e.at[0, lx - 1, :, 0:LANES]
        if msg == D2:
            return e.at[0, lx - 1, 0:ROWS, :]
        if msg == D3:
            return e.at[1, 0, ly - ROWS:ly, :]
        if msg == D4:
            return z_e.at[phase, ly - ROWS:ly, :]
        if msg == D5:
            return z_e.at[phase, 0:ROWS, :]
        return e.at[2, 0, :, lz - LANES:lz]

    def copy(msg, phase):
        return pltpu.make_async_remote_copy(
            src_ref=source(msg, phase), dst_ref=recv[msg].at[phase],
            send_sem=send_sem.at[phase, msg], recv_sem=recv_sem.at[phase, msg],
            device_id=at(OFFSETS[msg]), device_id_type=pl.DeviceIdType.MESH)

    def send(msg, phase):
        @pl.when(exists(OFFSETS[msg]))
        def _():
            copy(msg, phase).start()

    def wait_send(msg, phase):
        @pl.when(exists(OFFSETS[msg]))
        def _():
            copy(msg, phase).wait_send()

    def comes(msg):
        return exists(tuple(-o for o in OFFSETS[msg]))

    def wait_recv(msg, phase):
        @pl.when(comes(msg))
        def _():
            copy(msg, phase).wait_recv()

    for c in (1, 2):
        e_v[c, lx] = jnp.zeros((ly, lz), jnp.float32)

    for msg in range(12):
        @pl.when(jnp.logical_not(comes(msg)))
        def _(msg=msg):
            recv[msg][...] = jnp.zeros(recv[msg].shape, jnp.float32)

    row = lax.broadcasted_iota(jnp.int32, (ly, lz), 0)
    lane = lax.broadcasted_iota(jnp.int32, (ly, lz), 1)
    row1 = lax.broadcasted_iota(jnp.int32, (ly, LANES), 0)
    lane1 = lax.broadcasted_iota(jnp.int32, (ly, LANES), 1)

    def zup(v):
        return jnp.where(lane == lz - 1, 0.0, pltpu.roll(v, lz - 1, 1))

    def yup(v):
        return jnp.where(row == ly - 1, 0.0, pltpu.roll(v, ly - 1, 0))

    def pick(tile, from_lane, x, slot, acc):
        to = slot * lx + x
        shift = lax.rem(to + (LANES - from_lane), LANES)
        return jnp.where(lane1 == to, pltpu.roll(tile, shift, 1), acc)

    def place(packed, to_lane, x, slot):
        shift = lax.rem(2 * LANES + to_lane - (slot * lx + x), LANES)
        return pltpu.roll(packed, shift, 1)

    pl.semaphore_wait(barrier, count)
    for msg in (EX, D1, D2, D3, D6):
        send(msg, 0)

    plane = extent[1] * extent[2]
    port_x = []
    for p in range(nport):
        cell = ports[p]
        px = lax.div(cell, plane)
        rest = lax.rem(cell, plane)
        py = lax.div(rest, extent[2]) - start[1]
        pz = lax.rem(rest, extent[2]) - start[2]
        port_x.append(px - start[0])
        hit = (row == py) & (lane == pz)
        for s in range(STEPS):
            src_v[s, p] = jnp.where(hit, amps[s, p], 0.0)
    for s in range(STEPS):
        src_v[s, nport] = jnp.zeros((ly, lz), jnp.float32)

    loads[0].wait()

    def pack_e(x, ex, ey, ez, phase, acc):
        y_e[phase, 0, pl.ds(x, 1), :] = ex[0:1, :]
        y_e[phase, 1, pl.ds(x, 1), :] = ez[0:1, :]
        acc = pick(ex[:, 0:LANES], 0, x, 0, acc)
        acc = pick(ey[:, 0:LANES], 0, x, 1, acc)
        return pick(ez[:, lz - LANES:lz], LANES - 1, x, 2, acc)

    zero1 = jnp.zeros((ly, LANES), jnp.float32)

    def first_pack(x, acc):
        return pack_e(x, e_v[0, x], e_v[1, x], e_v[2, x], 0, acc)

    z_e[0] = lax.fori_loop(0, lx, first_pack, zero1, unroll=UP)
    for msg in (EY, EZ, D4, D5):
        send(msg, 0)
    loads[1].wait()

    def magnetic(phase):
        def one(x, acc):
            ex, ey, ez = e_v[0, x], e_v[1, x], e_v[2, x]
            dey, dez = e_v[1, x + 1] - ey, e_v[2, x + 1] - ez
            hx = h_v[0, x] - half * ((yup(ez) - ez) - (zup(ey) - ey))
            hy = h_v[1, x] - half * ((zup(ex) - ex) - dez)
            hz = h_v[2, x] - half * (dey - (yup(ex) - ex))
            h_v[0, x] = hx
            h_v[1, x] = hy
            h_v[2, x] = hz
            y_p[phase, 0, pl.ds(x, 1), :] = hx[ly - 1:ly, :]
            y_p[phase, 1, pl.ds(x, 1), :] = hz[ly - 1:ly, :]
            acc = pick(hx[:, lz - LANES:lz], LANES - 1, x, 0, acc)
            return pick(hy[:, lz - LANES:lz], LANES - 1, x, 1, acc)

        z_p[phase] = lax.fori_loop(0, lx, one, zero1, unroll=UM)

    flags = tuple((me[a] > 0).astype(jnp.float32) for a in range(3))

    def halos(phase):
        fx, fy, fz = flags
        d1 = pltpu.roll(r_d1[phase], LANES - 1, 1)
        d1 = jnp.concatenate([jnp.zeros((ly, lz - LANES), jnp.float32), d1], 1) if lz > LANES else d1
        x_h[0] = (r_px[phase, 0] + half * e_v[2, 0]) * fx - jnp.where(lane == lz - 1, half * d1, 0.0)
        d2 = jnp.broadcast_to(r_d2[phase, 0:1, :], (ly, lz))
        x_h[1] = (r_px[phase, 1] - half * e_v[1, 0]) * fx + jnp.where(row == ly - 1, half * d2, 0.0)
        d4 = jnp.broadcast_to(r_d4[phase, ROWS - 1:ROWS, :], (lx, LANES))
        rx = lax.broadcasted_iota(jnp.int32, (lx, LANES), 0)
        cx = lax.broadcasted_iota(jnp.int32, (lx, LANES), 1)
        d4 = jnp.sum(jnp.where(cx == rx + lx, d4, 0.0), axis=1, keepdims=True)
        ry = lax.broadcasted_iota(jnp.int32, (lx, lz), 0)
        cy = lax.broadcasted_iota(jnp.int32, (lx, lz), 1)
        y_h[0] = (r_py[phase, 0] - half * y_e[phase, 1]) * fy + jnp.where(cy == lz - 1, half * d4, 0.0)
        d3 = jnp.broadcast_to(r_d3[phase, ROWS - 1:ROWS, :], (lx, lz))
        y_h[1] = (r_py[phase, 1] + half * y_e[phase, 0]) * fy - jnp.where(ry == lx - 1, half * d3, 0.0)
        own = z_e[phase]
        fix = jnp.where(lane1 < lx, half * pltpu.roll(own, LANES - lx, 1), -half * pltpu.roll(own, lx, 1))
        zh = (r_pz[phase] + fix) * fz
        d5 = jnp.broadcast_to(pltpu.roll(r_d5[phase], LANES - 2 * lx, 1)[0:1, :], (ly, LANES))
        zh = zh - jnp.where((row1 == ly - 1) & (lane1 < lx), half * d5, 0.0)
        d6 = pltpu.roll(r_d6[phase], 2 * lx, 1)
        zh = zh + jnp.where(lane1 == 2 * lx - 1, half * d6, 0.0)
        h_v[1, lx - 1] = h_v[1, lx - 1] + half * r_ex[phase, 1]
        h_v[2, lx - 1] = h_v[2, lx - 1] - half * r_ex[phase, 0]
        return zh

    def pad_high(t):
        return jnp.concatenate([jnp.zeros((ly, lz - LANES), jnp.float32), t], 1) if lz > LANES else t

    def pad_low(t):
        return jnp.concatenate([t, jnp.zeros((ly, lz - LANES), jnp.float32)], 1) if lz > LANES else t

    def electric(step, zh):
        phase = step
        ze = r_ez[phase]

        def one(x, carry):
            hy_b, hz_b, acc = carry
            ex, ey, ez = e_v[0, x], e_v[1, x], e_v[2, x]
            top_row = row == ly - 1
            top_lane = lane == lz - 1
            eyz = pad_high(place(ze, LANES - 1, x, 1))
            exz = pad_high(place(ze, LANES - 1, x, 0))
            exy = jnp.broadcast_to(r_ey[phase, 0, pl.ds(x, 1), :], (ly, lz))
            ezy = jnp.broadcast_to(r_ey[phase, 1, pl.ds(x, 1), :], (ly, lz))
            hx = h_v[0, x] - jnp.where(top_row, half * ezy, 0.0) + jnp.where(top_lane, half * eyz, 0.0)
            hy = h_v[1, x] - jnp.where(top_lane, half * exz, 0.0)
            hz = h_v[2, x] + jnp.where(top_row, half * exy, 0.0)
            h_v[0, x] = hx
            h_v[1, x] = hy
            h_v[2, x] = hz
            low_row = row == 0
            low_lane = lane == 0
            hx_y = jnp.where(low_row, jnp.broadcast_to(y_h[0, pl.ds(x, 1), :], (ly, lz)), pltpu.roll(hx, 1, 0))
            hz_y = jnp.where(low_row, jnp.broadcast_to(y_h[1, pl.ds(x, 1), :], (ly, lz)), pltpu.roll(hz, 1, 0))
            hx_z = jnp.where(low_lane, pad_low(place(zh, 0, x, 0)), pltpu.roll(hx, 1, 1))
            hy_z = jnp.where(low_lane, pad_low(place(zh, 0, x, 1)), pltpu.roll(hy, 1, 1))
            c = c_v[x]
            ex = ex + c * ((hz - hz_y) - (hy - hy_z))
            ey = ey + c * ((hx - hx_z) - (hz - hz_b))
            ez = ez + c * ((hy - hy_b) - (hx - hx_y))
            for p in range(nport):
                ez = ez + src_v[step, jnp.where(port_x[p] == x, p, nport)]
            e_v[0, x] = ex
            e_v[1, x] = ey
            e_v[2, x] = ez
            total = None
            for comp, val in enumerate((ex, ey, ez)):
                change = s_v[step, comp, x].astype(jnp.float32) - s_v[step + 1, comp, x].astype(jnp.float32)
                t = val * change
                total = t if total is None else total + t
            fold = total[:, 0:LANES]
            for k in range(1, lz // LANES):
                fold = fold + total[:, k * LANES:(k + 1) * LANES]
            if step == 0:
                corr_v[x] = fold
            else:
                fold = fold + corr_v[x]
            if step + 1 < STEPS:
                acc = pack_e(x, ex, ey, ez, phase + 1, acc)
            else:
                acc = jnp.where(lane1 == x, jnp.sum(fold, axis=1, keepdims=True), acc)
            return hy, hz, acc

        _, _, acc = lax.fori_loop(0, lx, one, (x_h[0], x_h[1], zero1), unroll=UE)
        return acc

    magnetic(0)
    for msg in (PX, PY, PZ):
        send(msg, 0)

    loads[2].wait()
    coefs = [half / jnp.full((ly, lz), perm[k], jnp.float32) for k in range(nmat)]

    def coef_plane(x, carry):
        mat = m_v[x]
        c = coefs[0]
        for k in range(1, nmat):
            c = jnp.where(mat == k, coefs[k], c)
        c_v[x] = c
        return carry

    lax.fori_loop(0, lx, coef_plane, 0, unroll=UP)
    loads[3].wait()

    for step in range(STEPS):
        if step > 0:
            for msg in (EX, D1, D2, D3, D6, EY, EZ, D4, D5):
                send(msg, step)
            magnetic(step)
            for msg in (PX, PY, PZ):
                send(msg, step)
        for msg in range(12):
            wait_send(msg, step)
        for msg in range(12):
            wait_recv(msg, step)
        zh = halos(step)
        acc = electric(step, zh)
        if step + 1 < STEPS:
            z_e[step + 1] = acc

    own_rows = ly // nz_dev
    tile = g_out.shape[0]
    g_v[...] = acc
    g_v[:, 0:lx] = acc[:, 0:lx] * mask[...].astype(jnp.float32)

    def tile_of(k):
        return pl.ds(pl.multiple_of((k * own_rows) // tile * tile, ROWS), tile)

    gcopies = []
    for d in range(1, nz_dev):
        peer = lax.rem(me[2] + d, nz_dev)
        gcopies.append(pltpu.make_async_remote_copy(
            src_ref=g_v.at[tile_of(peer)], dst_ref=r_g.at[d - 1],
            send_sem=gs_sem.at[d - 1], recv_sem=gr_sem.at[d - 1],
            device_id=(me[0], me[1], peer), device_id_type=pl.DeviceIdType.MESH))
    for c in gcopies:
        c.start()
    total = g_v[tile_of(me[2])]
    for d, c in enumerate(gcopies):
        c.wait_recv()
        total = total + r_g[d]
    shift = lax.rem(tile - lax.rem(me[2] * own_rows, tile), tile)
    g_out[...] = pltpu.roll(total, shift, 0)
    for c in gcopies:
        c.wait_send()


def write_out(e_v, h_v, g_v, e_out, h_out, g_out, sem):
    lx = h_v.shape[1]
    outs = [
        pltpu.make_async_copy(e_v.at[:, 0:lx], e_out, sem.at[0]),
        pltpu.make_async_copy(h_v, h_out, sem.at[1]),
    ]
    for c in outs:
        c.start()
    g_out[...] = g_v[0:g_out.shape[0], 0:g_out.shape[1]]
    for c in outs:
        c.wait()


def solution(mesh):
    mesh_sizes = tuple(mesh.shape[a] for a in AXES)

    def body(e_adjoint, h_adjoint, snapshots, material, permittivity, design_mask, ports, amplitudes):
        _, lx, ly, lz = e_adjoint.shape
        extent = (lx * mesh_sizes[0], ly * mesh_sizes[1], lz * mesh_sizes[2])
        nport = ports.shape[0]
        f32 = jnp.float32
        own = ly // mesh_sizes[2]
        tile = max(ROWS, own)
        any_spec = pl.BlockSpec(memory_space=pl.ANY)
        smem = pl.BlockSpec(memory_space=pltpu.SMEM)
        vmem = pl.BlockSpec(memory_space=pltpu.VMEM)
        e, h, g = pl.pallas_call(
            lambda *refs: kernel(mesh_sizes, extent, *refs),
            out_shape=(
                pltpu.VMEM((3, lx + 1, ly, lz), f32),
                pltpu.VMEM((3, lx, ly, lz), f32),
                pltpu.VMEM((tile, LANES), f32),
            ),
            in_specs=[smem, smem, smem, vmem, any_spec, any_spec, any_spec, any_spec],
            out_specs=(vmem, vmem, vmem),
            scratch_shapes=[
                pltpu.VMEM(snapshots.shape, snapshots.dtype),
                pltpu.VMEM((lx, ly, lz), jnp.int32),
                pltpu.VMEM((lx, ly, lz), f32),
                pltpu.VMEM((lx, ly, LANES), f32),
                pltpu.VMEM((STEPS, nport + 1, ly, lz), f32),
                pltpu.VMEM((STEPS, 2, lx, lz), f32),
                pltpu.VMEM((STEPS, ly, LANES), f32),
                pltpu.VMEM((STEPS, 2, lx, lz), f32),
                pltpu.VMEM((STEPS, ly, LANES), f32),
                pltpu.VMEM((2, lx, lz), f32),
                pltpu.VMEM((2, ly, lz), f32),
                pltpu.VMEM((ly, LANES), f32),
                pltpu.VMEM((STEPS, 2, ly, lz), f32),
                pltpu.VMEM((STEPS, 2, lx, lz), f32),
                pltpu.VMEM((STEPS, ly, LANES), f32),
                pltpu.VMEM((STEPS, 2, ly, lz), f32),
                pltpu.VMEM((STEPS, 2, lx, lz), f32),
                pltpu.VMEM((STEPS, ly, LANES), f32),
                pltpu.VMEM((STEPS, ly, LANES), f32),
                pltpu.VMEM((STEPS, ROWS, lz), f32),
                pltpu.VMEM((STEPS, ROWS, lz), f32),
                pltpu.VMEM((STEPS, ROWS, LANES), f32),
                pltpu.VMEM((STEPS, ROWS, LANES), f32),
                pltpu.VMEM((STEPS, ly, LANES), f32),
                pltpu.VMEM((3, tile, LANES), f32),
                pltpu.SemaphoreType.DMA((4,)),
                pltpu.SemaphoreType.DMA((STEPS, 12)),
                pltpu.SemaphoreType.DMA((STEPS, 12)),
                pltpu.SemaphoreType.DMA((3,)),
                pltpu.SemaphoreType.DMA((3,)),
            ],
            compiler_params=pltpu.CompilerParams(collective_id=0, has_side_effects=True),
            name="reverse_steps",
        )(permittivity, ports, amplitudes, design_mask.T, e_adjoint, h_adjoint, snapshots, material)
        e, h, g = (pltpu.with_memory_space_constraint(v, pltpu.VMEM) for v in (e, h, g))
        e, h, g = pl.pallas_call(
            write_out,
            out_shape=(
                jax.ShapeDtypeStruct(e_adjoint.shape, f32),
                jax.ShapeDtypeStruct(h_adjoint.shape, f32),
                jax.ShapeDtypeStruct((own, lx), f32),
            ),
            in_specs=[vmem, vmem, vmem],
            out_specs=(any_spec, any_spec, vmem),
            scratch_shapes=[pltpu.SemaphoreType.DMA((2,))],
            name="write_out",
        )(e, h, g)
        return e, h, g.T

    placed = (
        P(None, "gx", "gy", "gz"),
        P(None, "gx", "gy", "gz"),
        P(None, None, "gx", "gy", "gz"),
        P("gx", "gy", "gz"),
        P(),
        P("gx", "gy"),
        P(),
        P(),
    )
    return jax.shard_map(
        body,
        mesh=mesh,
        in_specs=placed,
        out_specs=(P(None, "gx", "gy", "gz"), P(None, "gx", "gy", "gz"), P("gx", ("gy", "gz"))),
        check_vma=False,
    )
```

```python
import jax
import jax.numpy as jnp
from jax import lax
from jax.experimental import pallas as pl
from jax.experimental.pallas import tpu as pltpu
from jax.sharding import PartitionSpec as P

STEPS = 2
AXES = ("gx", "gy", "gz")
LANES = 128
ROWS = 8
half = 0.5
U_MAG, U_PRE, U_POST = 8, 8, 8
CHUNKS = 4

EX, EY, EZ, PX, PY, PZ, D1, D2, D3, D4, D5, D6 = range(12)
OFFSETS = (
    (-1, 0, 0), (0, -1, 0), (0, 0, -1),
    (1, 0, 0), (0, 1, 0), (0, 0, 1),
    (1, 0, -1), (1, -1, 0), (-1, 1, 0), (0, 1, -1), (0, -1, 1), (-1, 0, 1),
)


def kernel(mesh_sizes, extent, perm, ports, amps, mask, e_in, h_in, s_in, m_in,
           e_v, h_v, g_out,
           s_v, m_v, c_v, corr_v, diff_v, src_v,
           x_e, y_e, z_e, x_p, y_p, z_p, y_t, rows_v, g_v,
           r_ex, r_ey, r_ez, r_px, r_py, r_pz, r_d1, r_d2, r_d3, r_d4, r_d5, r_d6, r_g,
           in_sem, send_sem, recv_sem, gs_sem, gr_sem):
    _, lx, ly, lz = e_in.shape
    nt = lz // LANES
    off = 2 * lx
    f32 = jnp.float32
    nmat = perm.shape[0]
    nport = ports.shape[0]
    me = tuple(lax.axis_index(a) for a in AXES)
    start = (me[0] * lx, me[1] * ly, me[2] * lz)
    nz_dev = mesh_sizes[2]

    def exists(o):
        ok = None
        for a in range(3):
            if o[a] == 0:
                continue
            c = me[a] + o[a]
            t = (c >= 0) & (c < mesh_sizes[a])
            ok = t if ok is None else ok & t
        return ok

    def at(o):
        return tuple(me[a] + o[a] for a in range(3))

    step_x = lx // CHUNKS
    load_e, load_h = [], []
    for k in range(CHUNKS):
        d = pl.ds(k * step_x, step_x)
        load_e.append(pltpu.make_async_copy(e_in.at[:, d], e_v.at[:, d], in_sem.at[2 + k]))
        load_h.append(pltpu.make_async_copy(h_in.at[:, d], h_v.at[:, d], in_sem.at[2 + CHUNKS + k]))
    load_m = pltpu.make_async_copy(m_in, m_v, in_sem.at[0])
    load_s = pltpu.make_async_copy(s_in, s_v, in_sem.at[1])
    for c in load_e + load_h + [load_m, load_s]:
        c.start()

    barrier = pltpu.get_barrier_semaphore()
    count = jnp.int32(0)
    greet = list(OFFSETS)
    for d in range(2, nz_dev):
        greet += [(0, 0, d), (0, 0, -d)]
    for o in greet:
        ok = exists(o)
        count = count + ok.astype(jnp.int32)

        @pl.when(ok)
        def _(o=o):
            pl.semaphore_signal(barrier, inc=1, device_id=at(o), device_id_type=pl.DeviceIdType.MESH)

    recv = (r_ex, r_ey, r_ez, r_px, r_py, r_pz, r_d1, r_d2, r_d3, r_d4, r_d5, r_d6)

    def source(msg, phase):
        first = phase == 0
        if msg == EX:
            return e_in.at[1:3, 0] if first else x_e.at[phase, 0:2]
        if msg == EY:
            return y_e.at[phase]
        if msg == EZ:
            return z_e.at[phase]
        if msg == PX:
            return x_p.at[phase]
        if msg == PY:
            return y_p.at[phase]
        if msg == PZ:
            return z_p.at[phase]
        if msg == D1:
            return e_in.at[0, lx - 1, :, 0:LANES] if first else x_e.at[phase, 2, :, 0:LANES]
        if msg == D2:
            return e_in.at[0, lx - 1, 0:ROWS, :] if first else x_e.at[phase, 2, 0:ROWS, :]
        if msg == D3:
            return e_in.at[1, 0, ly - ROWS:ly, :] if first else x_e.at[phase, 0, ly - ROWS:ly, :]
        if msg == D4:
            return z_e.at[phase, ly - ROWS:ly, :]
        if msg == D5:
            return z_e.at[phase, 0:ROWS, :]
        return e_in.at[2, 0, :, lz - LANES:lz] if first else x_e.at[phase, 1, :, lz - LANES:lz]

    def copy(msg, phase):
        return pltpu.make_async_remote_copy(
            src_ref=source(msg, phase), dst_ref=recv[msg].at[phase],
            send_sem=send_sem.at[phase, msg], recv_sem=recv_sem.at[phase, msg],
            device_id=at(OFFSETS[msg]), device_id_type=pl.DeviceIdType.MESH)

    def send(msg, phase):
        @pl.when(exists(OFFSETS[msg]))
        def _():
            copy(msg, phase).start()

    def wait_send(msg, phase):
        @pl.when(exists(OFFSETS[msg]))
        def _():
            copy(msg, phase).wait_send()

    def comes(msg):
        return exists(tuple(-o for o in OFFSETS[msg]))

    def wait_recv(msg, phase):
        @pl.when(comes(msg))
        def _():
            copy(msg, phase).wait_recv()

    for c in (1, 2):
        e_v[c, lx] = jnp.zeros((ly, lz), f32)

    for msg in range(12):
        @pl.when(jnp.logical_not(comes(msg)))
        def _(msg=msg):
            recv[msg][...] = jnp.zeros(recv[msg].shape, f32)

    row = lax.broadcasted_iota(jnp.int32, (ly, lz), 0)
    lane = lax.broadcasted_iota(jnp.int32, (ly, lz), 1)
    row1 = lax.broadcasted_iota(jnp.int32, (ly, LANES), 0)
    lane1 = lax.broadcasted_iota(jnp.int32, (ly, LANES), 1)
    row8 = lax.broadcasted_iota(jnp.int32, (ROWS, LANES), 0)
    zero1 = jnp.zeros((ly, LANES), f32)

    def wide(t):
        return t[0] if nt == 1 else jnp.concatenate([t[k] for k in range(nt)], 1)

    def up(v, axis):
        n = v.shape[axis]
        i = lax.broadcasted_iota(jnp.int32, v.shape, axis)
        return jnp.where(i == n - 1, 0.0, pltpu.roll(v, n - 1, axis))

    def down(v, axis):
        i = lax.broadcasted_iota(jnp.int32, v.shape, axis)
        return jnp.where(i == 0, 0.0, pltpu.roll(v, 1, axis))

    def pick(tile, from_lane, to, acc):
        shift = lax.rem(to + (LANES - from_lane), LANES)
        return jnp.where(lane1 == to, pltpu.roll(tile, shift, 1), acc)

    def put_rows(dst, phase, comp, x, v, r):
        for k in range(nt):
            dst[phase, comp, k, pl.ds(x, 1), :] = v[r:r + 1, k * LANES:(k + 1) * LANES]

    def pack_top(x, phase, values):
        for i, v in enumerate(values):
            put_rows(y_t, phase, i, x, v, ly - 1)

    def pack_e(x, ex, ey, ez, phase, acc):
        put_rows(y_e, phase, 0, x, ex, 0)
        put_rows(y_e, phase, 1, x, ez, 0)
        acc = pick(ex[:, 0:LANES], 0, 2 * x, acc)
        acc = pick(ey[:, 0:LANES], 0, off + 2 * x, acc)
        return pick(ez[:, lz - LANES:lz], LANES - 1, 2 * x + 1, acc)

    def top_layers(phase):
        ex, ey, ez, hx, hz = (wide(y_t[phase, i]) for i in range(5))
        px = hx + half * (ez + (up(ey, 1) - ey))
        pz = hz - half * ((up(ey, 0) - ey) + ex)
        for i, v in enumerate((px, pz)):
            for k in range(nt):
                y_p[phase, i, k] = v[:, k * LANES:(k + 1) * LANES]
        ex, ey, ez = e_v[0, lx - 1], e_v[1, lx - 1], e_v[2, lx - 1]
        x_p[phase, 0] = h_v[1, lx - 1] - half * ((up(ex, 1) - ex) + ez)
        x_p[phase, 1] = h_v[2, lx - 1] + half * (ey + (up(ex, 0) - ex))

    def magnetic(phase):
        def one(x, acc):
            ex, ey, ez = e_v[0, x], e_v[1, x], e_v[2, x]
            dey, dez = e_v[1, x + 1] - ey, e_v[2, x + 1] - ez
            hx = h_v[0, x] - half * ((up(ez, 0) - ez) - (up(ey, 1) - ey))
            hy = h_v[1, x] - half * ((up(ex, 1) - ex) - dez)
            hz = h_v[2, x] - half * (dey - (up(ex, 0) - ex))
            h_v[0, x] = hx
            h_v[1, x] = hy
            h_v[2, x] = hz
            acc = pick(hy[:, lz - LANES:lz], LANES - 1, 2 * x + 1, acc)
            return pick(hx[:, lz - LANES:lz], LANES - 1, off + 2 * x + 1, acc)

        z_p[phase] = lax.fori_loop(0, lx, one, zero1, unroll=U_MAG)

    def save_e(phase):
        x_e[phase, 0] = e_v[1, 0]
        x_e[phase, 1] = e_v[2, 0]
        x_e[phase, 2] = e_v[0, lx - 1]

    def pre(step):
        def one(x, carry):
            hy_b, hz_b = carry
            ex, ey, ez = e_v[0, x], e_v[1, x], e_v[2, x]
            hx, hy, hz = h_v[0, x], h_v[1, x], h_v[2, x]
            if step == 0:
                mat = m_v[x]
                c = coefs[0]
                for k in range(1, nmat):
                    c = jnp.where(mat == k, coefs[k], c)
                c_v[x] = c
            else:
                c = c_v[x]
                total = None
                for comp, val in enumerate((ex, ey, ez)):
                    mid = s_v[step, comp, x].astype(f32)
                    t = val * (s_v[step - 1, comp, x].astype(f32) - mid)
                    total = t if total is None else total + t
                    diff_v[comp, x] = mid - s_v[step + 1, comp, x].astype(f32)
                fold = total[:, 0:LANES]
                for k in range(1, nt):
                    fold = fold + total[:, k * LANES:(k + 1) * LANES]
                corr_v[x] = fold
            e_v[0, x] = ex + c * ((hz - down(hz, 0)) - (hy - down(hy, 1)))
            e_v[1, x] = ey + c * ((hx - down(hx, 1)) - (hz - hz_b))
            ez = ez + c * ((hy - hy_b) - (hx - down(hx, 0)))
            for p in range(nport):
                ez = ez + src_v[step, jnp.where(port_x[p] == x, p, nport)]
            e_v[2, x] = ez
            return hy, hz

        zero = jnp.zeros((ly, lz), f32)
        lax.fori_loop(0, lx, one, (zero, zero), unroll=U_PRE)

    flags = tuple((me[a] > 0).astype(f32) for a in range(3))

    def pad_high(t):
        return jnp.concatenate([jnp.zeros((ly, lz - LANES), f32), t], 1) if lz > LANES else t

    def halos(phase):
        fx, fy, fz = flags
        d1 = pad_high(pltpu.roll(r_d1[phase], LANES - 1, 1))
        hy_x = (r_px[phase, 0] + half * x_e[phase, 1]) * fx - jnp.where(lane == lz - 1, half * d1, 0.0)
        d2 = jnp.broadcast_to(r_d2[phase, 0:1, :], (ly, lz))
        hz_x = (r_px[phase, 1] - half * x_e[phase, 0]) * fx + jnp.where(row == ly - 1, half * d2, 0.0)
        c0, c1 = c_v[0], c_v[lx - 1]
        e_v[1, 0] = e_v[1, 0] + c0 * hz_x
        e_v[2, 0] = e_v[2, 0] - c0 * hy_x
        dhy = half * r_ex[phase, 1]
        dhz = -half * r_ex[phase, 0]
        h_v[1, lx - 1] = h_v[1, lx - 1] + dhy
        h_v[2, lx - 1] = h_v[2, lx - 1] + dhz
        e_v[0, lx - 1] = e_v[0, lx - 1] + c1 * ((dhz - down(dhz, 0)) - (dhy - down(dhy, 1)))
        e_v[1, lx - 1] = e_v[1, lx - 1] - c1 * dhz
        e_v[2, lx - 1] = e_v[2, lx - 1] + c1 * dhy
        rx = lax.broadcasted_iota(jnp.int32, (lx, LANES), 0)
        cx = lax.broadcasted_iota(jnp.int32, (lx, LANES), 1)
        d4 = jnp.broadcast_to(r_d4[phase, ROWS - 1:ROWS, :], (lx, LANES))
        d4 = jnp.sum(jnp.where(cx == off + 2 * rx, d4, 0.0), axis=1, keepdims=True)
        ry = lax.broadcasted_iota(jnp.int32, (lx, lz), 0)
        cy = lax.broadcasted_iota(jnp.int32, (lx, lz), 1)
        hx_y = (wide(r_py[phase, 0]) - half * wide(y_e[phase, 1])) * fy + jnp.where(cy == lz - 1, half * d4, 0.0)
        d3 = jnp.broadcast_to(r_d3[phase, ROWS - 1:ROWS, :], (lx, lz))
        hz_y = (wide(r_py[phase, 1]) + half * wide(y_e[phase, 0])) * fy - jnp.where(ry == lx - 1, half * d3, 0.0)
        dhx = -half * wide(r_ey[phase, 1])
        dhz = half * wide(r_ey[phase, 0])
        values = (-hz_y, hx_y, dhz, (dhx - down(dhx, 1)) - (dhz - down(dhz, 0)), -dhx)
        for i, v in enumerate(values):
            for k in range(nt):
                rows_v[i, k] = v[:, k * LANES:(k + 1) * LANES]
        own = pltpu.roll(z_e[phase], 1, 1)
        low = lane1 < off
        zh = (r_pz[phase] + jnp.where(low, -half * own, half * own)) * fz
        d5 = jnp.broadcast_to(pltpu.roll(r_d5[phase], off, 1)[0:1, :], (ly, LANES))
        zh = zh - jnp.where((row1 == ly - 1) & (lane1 >= off), half * d5, 0.0)
        d6 = pltpu.roll(r_d6[phase], off, 1)
        zh = zh + jnp.where(lane1 == off - 1, half * d6, 0.0)
        ze = half * r_ez[phase]
        odd = lax.rem(lane1, 2) == 1
        cols = jnp.where(odd, jnp.where(low, zh, -zh), ze)
        dhy = jnp.where(odd | (lane1 >= off), 0.0, -ze)
        dhx = jnp.where(odd | (lane1 >= off), 0.0, pltpu.roll(ze, LANES - off, 1))
        shift_x = jnp.where(lane1 < 2, 0.0, pltpu.roll(dhy, 2, 1))
        last = (dhy - shift_x) - (dhx - down(dhx, 0))
        return cols, last

    top, bottom = row8 == 0, row8 == ROWS - 1
    lane8 = lax.broadcasted_iota(jnp.int32, (ROWS, LANES), 1)
    first_lane, last_lane = lane8 == 0, lane8 == LANES - 1
    nr = ly // ROWS

    def post(step, cols, last):
        def one(x, acc):
            low_col = pltpu.roll(cols, lax.rem(2 * LANES - (2 * x + 1), LANES), 1)
            high_col = pltpu.roll(cols, lax.rem(2 * LANES - (off + 2 * x + 1), LANES), 1)
            last_col = pltpu.roll(last, lax.rem(2 * LANES - (2 * x + 1), LANES), 1)
            def delta(r, k, col0, col1, row0, row1_):
                terms = []
                cut = slice(r * ROWS, (r + 1) * ROWS)
                if col0 is not None and k == 0:
                    terms.append(jnp.where(first_lane, col0[cut], 0.0))
                if col1 is not None and k == nt - 1:
                    terms.append(jnp.where(last_lane, col1[cut], 0.0))
                if row0 is not None and r == 0:
                    t = jnp.broadcast_to(rows_v[row0, k, pl.ds(x, 1), :], (ROWS, LANES))
                    terms.append(jnp.where(top, t, 0.0))
                if row1_ is not None and r == nr - 1:
                    t = jnp.broadcast_to(rows_v[row1_, k, pl.ds(x, 1), :], (ROWS, LANES))
                    terms.append(jnp.where(bottom, t, 0.0))
                return sum(terms[1:], terms[0]) if terms else None

            new = []
            for comp, args in enumerate(((low_col, low_col, 0, 2), (high_col, high_col, None, 3), (None, last_col, 1, 4))):
                strips = []
                for k in range(nt):
                    strip = []
                    for r in range(nr):
                        at_ = (comp, x, pl.ds(r * ROWS, ROWS), pl.ds(k * LANES, LANES))
                        d = delta(r, k, *args)
                        v = e_v[at_]
                        if d is not None:
                            v = v + c_v[x, r * ROWS:(r + 1) * ROWS, k * LANES:(k + 1) * LANES] * d
                            e_v[at_] = v
                        strip.append(v)
                    strips.append(jnp.concatenate(strip, 0) if nr > 1 else strip[0])
                new.append(strips)
            for comp, args in enumerate((
                ((None, high_col, None, None, 1), (None, None, None, 4, -1)),
                ((None, low_col, None, None, -1),),
                ((None, None, None, 2, 1),),
            )):
                for r in range(nr):
                    for k in range(nt):
                        at_ = (comp, x, pl.ds(r * ROWS, ROWS), pl.ds(k * LANES, LANES))
                        v = h_v[at_] if step + 1 < STEPS and r == nr - 1 and comp != 1 else None
                        for *which, sign in args:
                            d = delta(r, k, *which)
                            if d is not None:
                                v = h_v[at_] if v is None else v
                                v = v + d if sign > 0 else v - d
                        if v is not None:
                            h_v[at_] = v
                        if step + 1 < STEPS and r == nr - 1 and comp != 1:
                            y_t[step + 1, 3 + comp // 2, k, pl.ds(x, 1), :] = v[ROWS - 1:ROWS]
            if step + 1 < STEPS:
                values = [wide(n) for n in new]
                pack_top(x, step + 1, values)
                return pack_e(x, *values, step + 1, acc)
            fold = corr_v[x]
            for comp in range(3):
                for k in range(nt):
                    fold = fold + new[comp][k] * diff_v[comp, x, :, k * LANES:(k + 1) * LANES]
            return jnp.where(lane1 == x, jnp.sum(fold, axis=1, keepdims=True), acc)

        return lax.fori_loop(0, lx, one, zero1, unroll=U_POST)

    pl.semaphore_wait(barrier, count)
    for msg in (D2, D3, D1, D6, EX):
        send(msg, 0)

    def first_pack(x, acc):
        ex, ey, ez = e_v[0, x], e_v[1, x], e_v[2, x]
        pack_top(x, 0, (ex, ey, ez))
        return pack_e(x, ex, ey, ez, 0, acc)

    def first_top(x, carry):
        put_rows(y_t, 0, 3, x, h_v[0, x], ly - 1)
        put_rows(y_t, 0, 4, x, h_v[2, x], ly - 1)
        return carry

    acc = zero1
    for k in range(CHUNKS):
        load_e[k].wait()
        acc = lax.fori_loop(k * step_x, (k + 1) * step_x, first_pack, acc, unroll=True)
    z_e[0] = acc
    for msg in (EY, D4, D5, EZ):
        send(msg, 0)
    for k in range(CHUNKS):
        load_h[k].wait()
        lax.fori_loop(k * step_x, (k + 1) * step_x, first_top, 0, unroll=True)
    top_layers(0)
    send(PY, 0)
    send(PX, 0)
    magnetic(0)
    send(PZ, 0)
    save_e(0)

    plane = extent[1] * extent[2]
    port_x = []
    for p in range(nport):
        cell = ports[p]
        px = lax.div(cell, plane)
        rest = lax.rem(cell, plane)
        py = lax.div(rest, extent[2]) - start[1]
        pz = lax.rem(rest, extent[2]) - start[2]
        port_x.append(px - start[0])
        hit = (row == py) & (lane == pz)
        for s in range(STEPS):
            src_v[s, p] = jnp.where(hit, amps[s, p], 0.0)
    for s in range(STEPS):
        src_v[s, nport] = jnp.zeros((ly, lz), f32)
    coefs = [half / jnp.full((ly, lz), perm[k], f32) for k in range(nmat)]
    load_m.wait()
    pre(0)
    for msg in range(12):
        wait_recv(msg, 0)
    cols, last = halos(0)
    z_e[1] = post(0, cols, last)
    save_e(1)
    for msg in (D2, D3, D1, D6, D4, D5, EY, EX):
        send(msg, 1)
    top_layers(1)
    for msg in (PY, PX, EZ):
        send(msg, 1)
    magnetic(1)
    send(PZ, 1)
    load_s.wait()
    pre(1)
    for msg in range(12):
        wait_recv(msg, 1)
    cols, last = halos(1)
    acc = post(1, cols, last)

    own_rows = ly // nz_dev
    tile = g_out.shape[0]
    g_v[...] = acc
    g_v[:, 0:lx] = acc[:, 0:lx] * mask[...].astype(f32)

    def tile_of(k):
        return pl.ds(pl.multiple_of((k * own_rows) // tile * tile, ROWS), tile)

    gcopies = []
    for d in range(1, nz_dev):
        peer = lax.rem(me[2] + d, nz_dev)
        gcopies.append(pltpu.make_async_remote_copy(
            src_ref=g_v.at[tile_of(peer)], dst_ref=r_g.at[d - 1],
            send_sem=gs_sem.at[d - 1], recv_sem=gr_sem.at[d - 1],
            device_id=(me[0], me[1], peer), device_id_type=pl.DeviceIdType.MESH))
    for c in gcopies:
        c.start()
    for phase in range(STEPS):
        for msg in range(12):
            wait_send(msg, phase)
    total = g_v[tile_of(me[2])]
    for d, c in enumerate(gcopies):
        c.wait_recv()
        total = total + r_g[d]
    shift = lax.rem(tile - lax.rem(me[2] * own_rows, tile), tile)
    g_out[...] = pltpu.roll(total, shift, 0)
    for c in gcopies:
        c.wait_send()


def write_out(e_v, h_v, g_v, e_out, h_out, g_out, sem):
    lx = h_v.shape[1]
    outs = [
        pltpu.make_async_copy(e_v.at[:, 0:lx], e_out, sem.at[0]),
        pltpu.make_async_copy(h_v, h_out, sem.at[1]),
    ]
    for c in outs:
        c.start()
    g_out[...] = g_v[0:g_out.shape[0], 0:g_out.shape[1]]
    for c in outs:
        c.wait()


def solution(mesh):
    mesh_sizes = tuple(mesh.shape[a] for a in AXES)

    def body(e_adjoint, h_adjoint, snapshots, material, permittivity, design_mask, ports, amplitudes):
        _, lx, ly, lz = e_adjoint.shape
        extent = (lx * mesh_sizes[0], ly * mesh_sizes[1], lz * mesh_sizes[2])
        nport = ports.shape[0]
        nt = lz // LANES
        f32 = jnp.float32
        own = ly // mesh_sizes[2]
        tile = max(ROWS, own)
        any_spec = pl.BlockSpec(memory_space=pl.ANY)
        smem = pl.BlockSpec(memory_space=pltpu.SMEM)
        vmem = pl.BlockSpec(memory_space=pltpu.VMEM)
        e, h, g = pl.pallas_call(
            lambda *refs: kernel(mesh_sizes, extent, *refs),
            out_shape=(
                pltpu.VMEM((3, lx + 1, ly, lz), f32),
                pltpu.VMEM((3, lx, ly, lz), f32),
                pltpu.VMEM((tile, LANES), f32),
            ),
            in_specs=[smem, smem, smem, vmem, any_spec, any_spec, any_spec, any_spec],
            out_specs=(vmem, vmem, vmem),
            scratch_shapes=[
                pltpu.VMEM(snapshots.shape, snapshots.dtype),
                pltpu.VMEM((lx, ly, lz), jnp.int32),
                pltpu.VMEM((lx, ly, lz), f32),
                pltpu.VMEM((lx, ly, LANES), f32),
                pltpu.VMEM((3, lx, ly, lz), f32),
                pltpu.VMEM((STEPS, nport + 1, ly, lz), f32),
                pltpu.VMEM((STEPS, 3, ly, lz), f32),
                pltpu.VMEM((STEPS, 2, nt, lx, LANES), f32),
                pltpu.VMEM((STEPS, ly, LANES), f32),
                pltpu.VMEM((STEPS, 2, ly, lz), f32),
                pltpu.VMEM((STEPS, 2, nt, lx, LANES), f32),
                pltpu.VMEM((STEPS, ly, LANES), f32),
                pltpu.VMEM((STEPS, 5, nt, lx, LANES), f32),
                pltpu.VMEM((5, nt, lx, LANES), f32),
                pltpu.VMEM((ly, LANES), f32),
                pltpu.VMEM((STEPS, 2, ly, lz), f32),
                pltpu.VMEM((STEPS, 2, nt, lx, LANES), f32),
                pltpu.VMEM((STEPS, ly, LANES), f32),
                pltpu.VMEM((STEPS, 2, ly, lz), f32),
                pltpu.VMEM((STEPS, 2, nt, lx, LANES), f32),
                pltpu.VMEM((STEPS, ly, LANES), f32),
                pltpu.VMEM((STEPS, ly, LANES), f32),
                pltpu.VMEM((STEPS, ROWS, lz), f32),
                pltpu.VMEM((STEPS, ROWS, lz), f32),
                pltpu.VMEM((STEPS, ROWS, LANES), f32),
                pltpu.VMEM((STEPS, ROWS, LANES), f32),
                pltpu.VMEM((STEPS, ly, LANES), f32),
                pltpu.VMEM((3, tile, LANES), f32),
                pltpu.SemaphoreType.DMA((2 + 2 * CHUNKS,)),
                pltpu.SemaphoreType.DMA((STEPS, 12)),
                pltpu.SemaphoreType.DMA((STEPS, 12)),
                pltpu.SemaphoreType.DMA((3,)),
                pltpu.SemaphoreType.DMA((3,)),
            ],
            compiler_params=pltpu.CompilerParams(collective_id=0, has_side_effects=True),
            name="reverse_steps",
        )(permittivity, ports, amplitudes, design_mask.T, e_adjoint, h_adjoint, snapshots, material)
        e, h, g = (pltpu.with_memory_space_constraint(v, pltpu.VMEM) for v in (e, h, g))
        e, h, g = pl.pallas_call(
            write_out,
            out_shape=(
                jax.ShapeDtypeStruct(e_adjoint.shape, f32),
                jax.ShapeDtypeStruct(h_adjoint.shape, f32),
                jax.ShapeDtypeStruct((own, lx), f32),
            ),
            in_specs=[vmem, vmem, vmem],
            out_specs=(any_spec, any_spec, vmem),
            scratch_shapes=[pltpu.SemaphoreType.DMA((2,))],
            name="write_out",
        )(e, h, g)
        return e, h, g.T

    placed = (
        P(None, "gx", "gy", "gz"),
        P(None, "gx", "gy", "gz"),
        P(None, None, "gx", "gy", "gz"),
        P("gx", "gy", "gz"),
        P(),
        P("gx", "gy"),
        P(),
        P(),
    )
    return jax.shard_map(
        body,
        mesh=mesh,
        in_specs=placed,
        out_specs=(P(None, "gx", "gy", "gz"), P(None, "gx", "gy", "gz"), P("gx", ("gy", "gz"))),
        check_vma=False,
    )
```

```python
import jax
import jax.numpy as jnp
from jax import lax
from jax.experimental import pallas as pl
from jax.experimental.pallas import tpu as pltpu
from jax.sharding import PartitionSpec as P

STEPS = 2
AXES = ("gx", "gy", "gz")
LANES = 128
ROWS = 8
half = 0.5
U_MAG, U_PRE, U_POST, U_PACK = 8, 8, 8, 8

EX, EY, EZ, PX, PY, PZ, D1, D2, D3, D4, D5, D6 = range(12)
OFFSETS = (
    (-1, 0, 0), (0, -1, 0), (0, 0, -1),
    (1, 0, 0), (0, 1, 0), (0, 0, 1),
    (1, 0, -1), (1, -1, 0), (-1, 1, 0), (0, 1, -1), (0, -1, 1), (-1, 0, 1),
)


def kernel(mesh_sizes, extent, perm_in, ports_in, amps_in, mask_in, e_in, h_in, s_in, m_in,
           e_v, h_v, g_out,
           s_v, m_v, c_v, src_v,
           x_e, y_e, z_e, x_p, y_p, z_p, y_t, y_b, rows_v, g_v,
           r_ex, r_ey, r_ez, r_px, r_py, r_pz, r_d1, r_d2, r_d3, r_d4, r_d5, r_d6, r_g,
           perm, ports, amps, mask_v, in_sem, send_sem, recv_sem, gs_sem, gr_sem):
    _, lx, ly, lz = e_in.shape
    nt = lz // LANES
    off = 2 * lx
    f32 = jnp.float32
    nmat = perm_in.shape[0]
    nport = ports_in.shape[0]
    me = tuple(lax.axis_index(a) for a in AXES)
    start = (me[0] * lx, me[1] * ly, me[2] * lz)
    nz_dev = mesh_sizes[2]

    def exists(o):
        ok = None
        for a in range(3):
            if o[a] == 0:
                continue
            c = me[a] + o[a]
            t = (c >= 0) & (c < mesh_sizes[a])
            ok = t if ok is None else ok & t
        return ok

    def at(o):
        return tuple(me[a] + o[a] for a in range(3))

    high, low_part = pl.ds(ly - ROWS, ROWS), pl.ds(0, ly - ROWS)
    load_e, load_h = [], []
    for k, d in enumerate((high, low_part)):
        load_e.append(pltpu.make_async_copy(e_in.at[:, :, d], e_v.at[:, 0:lx, d], in_sem.at[2 + 2 * k]))
        load_h.append(pltpu.make_async_copy(h_in.at[:, :, d], h_v.at[:, :, d], in_sem.at[3 + 2 * k]))
    load_m = pltpu.make_async_copy(m_in, m_v, in_sem.at[0])
    load_s = pltpu.make_async_copy(s_in, s_v, in_sem.at[1])
    load_small = [
        pltpu.make_async_copy(a, b, in_sem.at[6 + i])
        for i, (a, b) in enumerate(((perm_in, perm), (ports_in, ports), (amps_in, amps), (mask_in, mask_v)))
    ]
    for c in [load_e[0], load_h[0], load_e[1], load_h[1]] + load_small + [load_m, load_s]:
        c.start()

    barrier = pltpu.get_barrier_semaphore()
    count = jnp.int32(0)
    greet = list(OFFSETS)
    for d in range(2, nz_dev):
        greet += [(0, 0, d), (0, 0, -d)]
    for o in greet:
        ok = exists(o)
        count = count + ok.astype(jnp.int32)

        @pl.when(ok)
        def _(o=o):
            pl.semaphore_signal(barrier, inc=1, device_id=at(o), device_id_type=pl.DeviceIdType.MESH)

    recv = (r_ex, r_ey, r_ez, r_px, r_py, r_pz, r_d1, r_d2, r_d3, r_d4, r_d5, r_d6)

    def source(msg, phase):
        first = phase == 0
        if msg == EX:
            return e_in.at[1:3, 0] if first else x_e.at[phase, 0:2]
        if msg == EY:
            return y_e.at[phase]
        if msg == EZ:
            return z_e.at[phase]
        if msg == PX:
            return x_p.at[phase]
        if msg == PY:
            return y_p.at[phase]
        if msg == PZ:
            return z_p.at[phase]
        if msg == D1:
            return e_in.at[0, lx - 1, :, 0:LANES] if first else x_e.at[phase, 2, :, 0:LANES]
        if msg == D2:
            return e_in.at[0, lx - 1, 0:ROWS, :] if first else x_e.at[phase, 2, 0:ROWS, :]
        if msg == D3:
            return e_in.at[1, 0, ly - ROWS:ly, :] if first else x_e.at[phase, 0, ly - ROWS:ly, :]
        if msg == D4:
            return z_e.at[phase, ly - ROWS:ly, :]
        if msg == D5:
            return z_e.at[phase, 0:ROWS, :]
        return e_in.at[2, 0, :, lz - LANES:lz] if first else x_e.at[phase, 1, :, lz - LANES:lz]

    def copy(msg, phase):
        return pltpu.make_async_remote_copy(
            src_ref=source(msg, phase), dst_ref=recv[msg].at[phase],
            send_sem=send_sem.at[phase, msg], recv_sem=recv_sem.at[phase, msg],
            device_id=at(OFFSETS[msg]), device_id_type=pl.DeviceIdType.MESH)

    def send(msg, phase):
        @pl.when(exists(OFFSETS[msg]))
        def _():
            copy(msg, phase).start()

    def wait_send(msg, phase):
        @pl.when(exists(OFFSETS[msg]))
        def _():
            copy(msg, phase).wait_send()

    def comes(msg):
        return exists(tuple(-o for o in OFFSETS[msg]))

    def wait_recv(msg, phase):
        @pl.when(comes(msg))
        def _():
            copy(msg, phase).wait_recv()

    for c in (1, 2):
        e_v[c, lx] = jnp.zeros((ly, lz), f32)

    for msg in range(12):
        @pl.when(jnp.logical_not(comes(msg)))
        def _(msg=msg):
            recv[msg][...] = jnp.zeros(recv[msg].shape, f32)

    row = lax.broadcasted_iota(jnp.int32, (ly, lz), 0)
    lane = lax.broadcasted_iota(jnp.int32, (ly, lz), 1)
    row1 = lax.broadcasted_iota(jnp.int32, (ly, LANES), 0)
    lane1 = lax.broadcasted_iota(jnp.int32, (ly, LANES), 1)
    row8 = lax.broadcasted_iota(jnp.int32, (ROWS, LANES), 0)
    zero1 = jnp.zeros((ly, LANES), f32)

    def wide(t):
        return t[0] if nt == 1 else jnp.concatenate([t[k] for k in range(nt)], 1)

    def up(v, axis):
        n = v.shape[axis]
        i = lax.broadcasted_iota(jnp.int32, v.shape, axis)
        return jnp.where(i == n - 1, 0.0, pltpu.roll(v, n - 1, axis))

    def down(v, axis):
        i = lax.broadcasted_iota(jnp.int32, v.shape, axis)
        return jnp.where(i == 0, 0.0, pltpu.roll(v, 1, axis))

    def pick(tile, from_lane, to, acc):
        shift = lax.rem(to + (LANES - from_lane), LANES)
        return jnp.where(lane1 == to, pltpu.roll(tile, shift, 1), acc)

    def put(dst, i, x, v, r):
        for k in range(nt):
            dst[i, k, pl.ds(x, 1), :] = v[r:r + 1, k * LANES:(k + 1) * LANES]

    def put_wide(dst, i, v):
        for k in range(nt):
            dst[i, k] = v[:, k * LANES:(k + 1) * LANES]

    def pick_e(x, ex, ey, ez, acc):
        acc = pick(ex[:, 0:LANES], 0, 2 * x, acc)
        acc = pick(ey[:, 0:LANES], 0, off + 2 * x, acc)
        return pick(ez[:, lz - LANES:lz], LANES - 1, 2 * x + 1, acc)

    def top_y(phase, ex, ey, ez, hx, hz):
        put_wide(y_p.at[phase], 0, hx + half * (ez + (up(ey, 1) - ey)))
        put_wide(y_p.at[phase], 1, hz - half * ((up(ey, 0) - ey) + ex))

    def top_x(phase):
        ex, ey, ez = e_v[0, lx - 1], e_v[1, lx - 1], e_v[2, lx - 1]
        x_p[phase, 0] = h_v[1, lx - 1] - half * ((up(ex, 1) - ex) + ez)
        x_p[phase, 1] = h_v[2, lx - 1] + half * (ey + (up(ex, 0) - ex))

    def magnetic(phase):
        def one(x, acc):
            ex, ey, ez = e_v[0, x], e_v[1, x], e_v[2, x]
            dey, dez = e_v[1, x + 1] - ey, e_v[2, x + 1] - ez
            hx = h_v[0, x] - half * ((up(ez, 0) - ez) - (up(ey, 1) - ey))
            hy = h_v[1, x] - half * ((up(ex, 1) - ex) - dez)
            hz = h_v[2, x] - half * (dey - (up(ex, 0) - ex))
            h_v[0, x] = hx
            h_v[1, x] = hy
            h_v[2, x] = hz
            acc = pick(hy[:, lz - LANES:lz], LANES - 1, 2 * x + 1, acc)
            return pick(hx[:, lz - LANES:lz], LANES - 1, off + 2 * x + 1, acc)

        z_p[phase] = lax.fori_loop(0, lx, one, zero1, unroll=U_MAG)

    def save_e(phase):
        x_e[phase, 0] = e_v[1, 0]
        x_e[phase, 1] = e_v[2, 0]
        x_e[phase, 2] = e_v[0, lx - 1]

    def pre(step):
        def one(x, carry):
            hy_b, hz_b, acc_c, acc_l, acc_g = carry
            ex, ey, ez = e_v[0, x], e_v[1, x], e_v[2, x]
            hx, hy, hz = h_v[0, x], h_v[1, x], h_v[2, x]
            if step == 0:
                mat = m_v[x]
                c = coefs[0]
                for k in range(1, nmat):
                    c = jnp.where(mat == k, coefs[k], c)
                c_v[x] = c
            else:
                c = c_v[x]
                total, change = None, []
                for comp, val in enumerate((ex, ey, ez)):
                    mid = s_v[step, comp, x].astype(f32)
                    t = val * (s_v[step - 1, comp, x].astype(f32) - mid)
                    total = t if total is None else total + t
                    change.append(mid - s_v[step + 1, comp, x].astype(f32))
            ex = ex + c * ((hz - down(hz, 0)) - (hy - down(hy, 1)))
            ey = ey + c * ((hx - down(hx, 1)) - (hz - hz_b))
            ez = ez + c * ((hy - hy_b) - (hx - down(hx, 0)))
            for p in range(nport):
                ez = ez + src_v[step, jnp.where(port_x[p] == x, p, nport)]
            e_v[0, x] = ex
            e_v[1, x] = ey
            e_v[2, x] = ez
            if step == 0:
                for i, (v, r) in enumerate(((ex, 0), (ez, 0), (ex, -1), (ey, -1), (ez, -1), (hx, -1), (hz, -1), (c, 0), (c, -1))):
                    put(y_b, i, x, v, r % ly)
            else:
                for val, d in zip((ex, ey, ez), change):
                    total = total + val * d
                fold = total[:, 0:LANES]
                for k in range(1, nt):
                    fold = fold + total[:, k * LANES:(k + 1) * LANES]
                acc_g = jnp.where(lane1 == 2 * x, jnp.sum(fold, axis=1, keepdims=True), acc_g)
                wx, wy, wz = (c * d for d in change)
                for i, (v, r) in enumerate(((wx, 0), (wz, 0), (wx, -1), (wy, -1), (wz, -1))):
                    put(y_b, i, x, v, r % ly)
                acc_c = pick(wx[:, 0:LANES], 0, 2 * x + 1, acc_c)
                acc_c = pick(wy[:, 0:LANES], 0, off + 2 * x + 1, acc_c)
                acc_c = pick(wx[:, lz - LANES:lz], LANES - 1, 2 * x, acc_c)
                acc_c = pick(wy[:, lz - LANES:lz], LANES - 1, off + 2 * x, acc_c)
                acc_l = pick(wz[:, lz - LANES:lz], LANES - 1, 2 * x, acc_l)
            return hy, hz, acc_c, acc_l, acc_g

        zero = jnp.zeros((ly, lz), f32)
        return lax.fori_loop(0, lx, one, (zero, zero, zero1, zero1, zero1), unroll=U_PRE)[2:]

    flags = tuple((me[a] > 0).astype(f32) for a in range(3))

    def pad_high(t):
        return jnp.concatenate([jnp.zeros((ly, lz - LANES), f32), t], 1) if lz > LANES else t

    def halos(phase):
        fx, fy, fz = flags
        d1 = pad_high(pltpu.roll(r_d1[phase], LANES - 1, 1))
        hy_x = (r_px[phase, 0] + half * x_e[phase, 1]) * fx - jnp.where(lane == lz - 1, half * d1, 0.0)
        d2 = jnp.broadcast_to(r_d2[phase, 0:1, :], (ly, lz))
        hz_x = (r_px[phase, 1] - half * x_e[phase, 0]) * fx + jnp.where(row == ly - 1, half * d2, 0.0)
        c0, c1 = c_v[0], c_v[lx - 1]
        dhy = half * r_ex[phase, 1]
        dhz = -half * r_ex[phase, 0]
        h_v[1, lx - 1] = h_v[1, lx - 1] + dhy
        h_v[2, lx - 1] = h_v[2, lx - 1] + dhz
        planes = (
            (1, 0, c0 * hz_x), (2, 0, -c0 * hy_x),
            (0, lx - 1, c1 * ((dhz - down(dhz, 0)) - (dhy - down(dhy, 1)))),
            (1, lx - 1, -c1 * dhz), (2, lx - 1, c1 * dhy),
        )
        for comp, x, d in planes:
            e_v[comp, x] = e_v[comp, x] + d
        rx = lax.broadcasted_iota(jnp.int32, (lx, LANES), 0)
        cx = lax.broadcasted_iota(jnp.int32, (lx, LANES), 1)
        d4 = jnp.broadcast_to(r_d4[phase, ROWS - 1:ROWS, :], (lx, LANES))
        d4 = jnp.sum(jnp.where(cx == off + 2 * rx, d4, 0.0), axis=1, keepdims=True)
        ry = lax.broadcasted_iota(jnp.int32, (lx, lz), 0)
        cy = lax.broadcasted_iota(jnp.int32, (lx, lz), 1)
        hx_y = (wide(r_py[phase, 0]) - half * wide(y_e[phase, 1])) * fy + jnp.where(cy == lz - 1, half * d4, 0.0)
        d3 = jnp.broadcast_to(r_d3[phase, ROWS - 1:ROWS, :], (lx, lz))
        hz_y = (wide(r_py[phase, 1]) + half * wide(y_e[phase, 0])) * fy - jnp.where(ry == lx - 1, half * d3, 0.0)
        dhx = -half * wide(r_ey[phase, 1])
        dhz = half * wide(r_ey[phase, 0])
        values = (-hz_y, hx_y, dhz, (dhx - down(dhx, 1)) - (dhz - down(dhz, 0)), -dhx)
        for i, v in enumerate(values):
            put_wide(rows_v, i, v)
        own = pltpu.roll(z_e[phase], 1, 1)
        low = lane1 < off
        zh = (r_pz[phase] + jnp.where(low, -half * own, half * own)) * fz
        d5 = jnp.broadcast_to(pltpu.roll(r_d5[phase], off, 1)[0:1, :], (ly, LANES))
        zh = zh - jnp.where((row1 == ly - 1) & (lane1 >= off), half * d5, 0.0)
        d6 = pltpu.roll(r_d6[phase], off, 1)
        zh = zh + jnp.where(lane1 == off - 1, half * d6, 0.0)
        ze = half * r_ez[phase]
        odd = lax.rem(lane1, 2) == 1
        cols = jnp.where(odd, jnp.where(low, zh, -zh), ze)
        dhy = jnp.where(odd | (lane1 >= off), 0.0, -ze)
        dhx = jnp.where(odd | (lane1 >= off), 0.0, pltpu.roll(ze, LANES - off, 1))
        shift_x = jnp.where(lane1 < 2, 0.0, pltpu.roll(dhy, 2, 1))
        last = (dhy - shift_x) - (dhx - down(dhx, 0))
        return planes, values, cols, last

    rx1 = lax.broadcasted_iota(jnp.int32, (lx, LANES), 0)
    cx1 = lax.broadcasted_iota(jnp.int32, (lx, LANES), 1)
    cyw = lax.broadcasted_iota(jnp.int32, (lx, lz), 1)

    def first_rows(values, cols, last):
        for x in (0, lx - 1):
            for i, (src, comp, r) in enumerate((
                (e_v, 0, 0), (e_v, 2, 0), (e_v, 0, -1), (e_v, 1, -1), (e_v, 2, -1), (h_v, 0, -1), (h_v, 2, -1))):
                put(y_b, i, x, src[comp, x], r % ly)

        def edge(col, y, at_lane, to):
            t = jnp.where(cx1 == 2 * rx1 + at_lane, jnp.broadcast_to(col[y:y + 1], (lx, LANES)), 0.0)
            return jnp.where(cyw == to, jnp.sum(t, axis=1, keepdims=True), 0.0)

        b = [wide(y_b[i]) for i in range(9)]
        y, end = ly - 1, lz - 1
        hx_edge = edge(cols, y, off, end)
        put_wide(y_e.at[1], 0, b[0] + b[7] * (values[0] + edge(cols, 0, 1, 0) + edge(cols, 0, 0, end)))
        put_wide(y_e.at[1], 1, b[1] + b[7] * (values[1] + edge(last, 0, 0, end)))
        ex = b[2] + b[8] * (values[2] + edge(cols, y, 1, 0) + edge(cols, y, 0, end))
        ey = b[3] + b[8] * (values[3] + edge(cols, y, off + 1, 0) + hx_edge)
        ez = b[4] + b[8] * (values[4] + edge(last, y, 0, end))
        top_y(1, ex, ey, ez, b[5] - values[4] + hx_edge, b[6] + values[2])

    def gradient_part(planes, values, cols, last, acc_c, acc_l, acc_g):
        w = [wide(y_b[i]) for i in range(5)]
        total = acc_g
        for y, t in ((0, values[0] * w[0] + values[1] * w[1]), (ly - 1, values[2] * w[2] + values[3] * w[3] + values[4] * w[4])):
            t = jnp.sum(t, axis=1, keepdims=True)
            t = jnp.sum(jnp.where(cx1 == 2 * rx1, t, 0.0), axis=0, keepdims=True)
            total = total + jnp.where(row1 == y, t, 0.0)
        p = cols * acc_c
        q = p + pltpu.roll(p, LANES - 1, 1)
        q = q + pltpu.roll(q, LANES - off, 1) + last * acc_l
        total = total + jnp.where((lane1 < off) & (lax.rem(lane1, 2) == 0), q, 0.0)
        for x in (0, lx - 1):
            t = None
            for comp, at_x, d in planes:
                if at_x == x:
                    change = s_v[STEPS - 1, comp, x].astype(f32) - s_v[STEPS, comp, x].astype(f32)
                    t = d * change if t is None else t + d * change
            total = total + jnp.where(lane1 == 2 * x, jnp.sum(t, axis=1, keepdims=True), 0.0)
        return total

    top, bottom = row8 == 0, row8 == ROWS - 1
    lane8 = lax.broadcasted_iota(jnp.int32, (ROWS, LANES), 1)
    first_lane, last_lane = lane8 == 0, lane8 == LANES - 1
    nr = ly // ROWS

    def post(step, cols, last):
        def one(x, acc):
            low_col = pltpu.roll(cols, lax.rem(2 * LANES - (2 * x + 1), LANES), 1)
            high_col = pltpu.roll(cols, lax.rem(2 * LANES - (off + 2 * x + 1), LANES), 1)
            last_col = pltpu.roll(last, lax.rem(2 * LANES - (2 * x + 1), LANES), 1)
            def delta(r, k, col0, col1, row0, row1_):
                terms = []
                cut = slice(r * ROWS, (r + 1) * ROWS)
                if col0 is not None and k == 0:
                    terms.append(jnp.where(first_lane, col0[cut], 0.0))
                if col1 is not None and k == nt - 1:
                    terms.append(jnp.where(last_lane, col1[cut], 0.0))
                if row0 is not None and r == 0:
                    t = jnp.broadcast_to(rows_v[row0, k, pl.ds(x, 1), :], (ROWS, LANES))
                    terms.append(jnp.where(top, t, 0.0))
                if row1_ is not None and r == nr - 1:
                    t = jnp.broadcast_to(rows_v[row1_, k, pl.ds(x, 1), :], (ROWS, LANES))
                    terms.append(jnp.where(bottom, t, 0.0))
                return sum(terms[1:], terms[0]) if terms else None

            new = []
            for comp, args in enumerate(((low_col, low_col, 0, 2), (high_col, high_col, None, 3), (None, last_col, 1, 4))):
                strips = []
                for k in range(nt):
                    strip = []
                    for r in range(nr):
                        at_ = (comp, x, pl.ds(r * ROWS, ROWS), pl.ds(k * LANES, LANES))
                        d = delta(r, k, *args)
                        v = e_v[at_]
                        if d is not None:
                            v = v + c_v[x, r * ROWS:(r + 1) * ROWS, k * LANES:(k + 1) * LANES] * d
                            e_v[at_] = v
                        strip.append(v)
                    strips.append(jnp.concatenate(strip, 0) if nr > 1 else strip[0])
                new.append(strips)
            for comp, args in enumerate((
                ((None, high_col, None, None, 1), (None, None, None, 4, -1)),
                ((None, low_col, None, None, -1),),
                ((None, None, None, 2, 1),),
            )):
                for r in range(nr):
                    for k in range(nt):
                        at_ = (comp, x, pl.ds(r * ROWS, ROWS), pl.ds(k * LANES, LANES))
                        v = None
                        for *which, sign in args:
                            d = delta(r, k, *which)
                            if d is not None:
                                v = h_v[at_] if v is None else v
                                v = v + d if sign > 0 else v - d
                        if v is not None:
                            h_v[at_] = v
            return pick_e(x, *(wide(n) for n in new), acc) if step + 1 < STEPS else acc

        return lax.fori_loop(0, lx, one, zero1, unroll=U_POST)

    pl.semaphore_wait(barrier, count)
    for msg in (D2, D3, D1, D6, EX):
        send(msg, 0)

    def first_top(x, carry):
        for i, (src, comp) in enumerate(((e_v, 0), (e_v, 1), (e_v, 2), (h_v, 0), (h_v, 2))):
            put(y_t, i, x, src[comp, x, ly - ROWS:ly, :], ROWS - 1)
        return carry

    def first_pack(x, acc):
        ex, ey, ez = e_v[0, x], e_v[1, x], e_v[2, x]
        put(y_e.at[0], 0, x, ex, 0)
        put(y_e.at[0], 1, x, ez, 0)
        return pick_e(x, ex, ey, ez, acc)

    load_e[0].wait()
    load_h[0].wait()
    lax.fori_loop(0, lx, first_top, 0, unroll=U_PACK)
    top_y(0, *(wide(y_t[i]) for i in range(5)))
    send(PY, 0)
    load_e[1].wait()
    z_e[0] = lax.fori_loop(0, lx, first_pack, zero1, unroll=U_PACK)
    for msg in (EY, D4, D5, EZ):
        send(msg, 0)
    load_h[1].wait()
    top_x(0)
    send(PX, 0)
    magnetic(0)
    send(PZ, 0)
    save_e(0)

    for c in load_small:
        c.wait()
    plane = extent[1] * extent[2]
    port_x = []
    for p in range(nport):
        cell = ports[p]
        px = lax.div(cell, plane)
        rest = lax.rem(cell, plane)
        py = lax.div(rest, extent[2]) - start[1]
        pz = lax.rem(rest, extent[2]) - start[2]
        port_x.append(px - start[0])
        hit = (row == py) & (lane == pz)
        for s in range(STEPS):
            src_v[s, p] = jnp.where(hit, amps[s, p], 0.0)
    for s in range(STEPS):
        src_v[s, nport] = jnp.zeros((ly, lz), f32)
    coefs = [half / jnp.full((ly, lz), perm[k], f32) for k in range(nmat)]
    load_m.wait()
    pre(0)
    for msg in range(12):
        wait_recv(msg, 0)
    planes, values, cols, last = halos(0)
    first_rows(values, cols, last)
    for msg in (EY, PY):
        send(msg, 1)
    z_e[1] = post(0, cols, last)
    save_e(1)
    for msg in (D2, D3, D1, D6, D4, D5, EX):
        send(msg, 1)
    top_x(1)
    for msg in (PX, EZ):
        send(msg, 1)
    magnetic(1)
    send(PZ, 1)
    load_s.wait()
    weights = pre(1)
    spread = lax.broadcasted_iota(jnp.int32, (lx, LANES), 1) == 2 * lax.broadcasted_iota(jnp.int32, (lx, LANES), 0)
    mask = jnp.dot(mask_v[...].astype(f32), spread.astype(f32), preferred_element_type=f32)
    for msg in range(12):
        wait_recv(msg, 1)
    planes, values, cols, last = halos(1)
    acc = gradient_part(planes, values, cols, last, *weights)

    own_rows = ly // nz_dev
    tile = g_out.shape[0]
    g_v[...] = acc * mask

    def tile_of(k):
        return pl.ds(pl.multiple_of((k * own_rows) // tile * tile, ROWS), tile)

    gcopies = []
    for d in range(1, nz_dev):
        peer = lax.rem(me[2] + d, nz_dev)
        gcopies.append(pltpu.make_async_remote_copy(
            src_ref=g_v.at[tile_of(peer)], dst_ref=r_g.at[d - 1],
            send_sem=gs_sem.at[d - 1], recv_sem=gr_sem.at[d - 1],
            device_id=(me[0], me[1], peer), device_id_type=pl.DeviceIdType.MESH))
    for c in gcopies:
        c.start()
    post(1, cols, last)
    for phase in range(STEPS):
        for msg in range(12):
            wait_send(msg, phase)
    total = g_v[tile_of(me[2])]
    for d, c in enumerate(gcopies):
        c.wait_recv()
        total = total + r_g[d]
    shift = lax.rem(tile - lax.rem(me[2] * own_rows, tile), tile)
    g_out[...] = pltpu.roll(total, shift, 0)
    for c in gcopies:
        c.wait_send()


def write_out(e_v, h_v, g_v, e_out, h_out, g_out, sem):
    lx = h_v.shape[1]
    outs = [
        pltpu.make_async_copy(e_v.at[:, 0:lx], e_out, sem.at[0]),
        pltpu.make_async_copy(h_v, h_out, sem.at[1]),
    ]
    for c in outs:
        c.start()
    own, _ = g_out.shape
    pick = lax.broadcasted_iota(jnp.int32, (LANES, LANES), 0) == 2 * lax.broadcasted_iota(jnp.int32, (LANES, LANES), 1)
    g = jnp.dot(g_v[...], pick.astype(jnp.float32), precision=lax.Precision.HIGHEST, preferred_element_type=jnp.float32)
    g_out[...] = g[0:own, 0:lx]
    for c in outs:
        c.wait()


def solution(mesh):
    mesh_sizes = tuple(mesh.shape[a] for a in AXES)

    def body(e_adjoint, h_adjoint, snapshots, material, permittivity, design_mask, ports, amplitudes):
        _, lx, ly, lz = e_adjoint.shape
        extent = (lx * mesh_sizes[0], ly * mesh_sizes[1], lz * mesh_sizes[2])
        nport = ports.shape[0]
        nt = lz // LANES
        f32 = jnp.float32
        own = ly // mesh_sizes[2]
        tile = max(ROWS, own)
        any_spec = pl.BlockSpec(memory_space=pl.ANY)
        vmem = pl.BlockSpec(memory_space=pltpu.VMEM)
        e, h, g = pl.pallas_call(
            lambda *refs: kernel(mesh_sizes, extent, *refs),
            out_shape=(
                pltpu.VMEM((3, lx + 1, ly, lz), f32),
                pltpu.VMEM((3, lx, ly, lz), f32),
                pltpu.VMEM((tile, LANES), f32),
            ),
            in_specs=[any_spec, any_spec, any_spec, any_spec, any_spec, any_spec, any_spec, any_spec],
            out_specs=(vmem, vmem, vmem),
            scratch_shapes=[
                pltpu.VMEM(snapshots.shape, snapshots.dtype),
                pltpu.VMEM((lx, ly, lz), jnp.int32),
                pltpu.VMEM((lx, ly, lz), f32),
                pltpu.VMEM((STEPS, nport + 1, ly, lz), f32),
                pltpu.VMEM((STEPS, 3, ly, lz), f32),
                pltpu.VMEM((STEPS, 2, nt, lx, LANES), f32),
                pltpu.VMEM((STEPS, ly, LANES), f32),
                pltpu.VMEM((STEPS, 2, ly, lz), f32),
                pltpu.VMEM((STEPS, 2, nt, lx, LANES), f32),
                pltpu.VMEM((STEPS, ly, LANES), f32),
                pltpu.VMEM((5, nt, lx, LANES), f32),
                pltpu.VMEM((9, nt, lx, LANES), f32),
                pltpu.VMEM((5, nt, lx, LANES), f32),
                pltpu.VMEM((ly, LANES), f32),
                pltpu.VMEM((STEPS, 2, ly, lz), f32),
                pltpu.VMEM((STEPS, 2, nt, lx, LANES), f32),
                pltpu.VMEM((STEPS, ly, LANES), f32),
                pltpu.VMEM((STEPS, 2, ly, lz), f32),
                pltpu.VMEM((STEPS, 2, nt, lx, LANES), f32),
                pltpu.VMEM((STEPS, ly, LANES), f32),
                pltpu.VMEM((STEPS, ly, LANES), f32),
                pltpu.VMEM((STEPS, ROWS, lz), f32),
                pltpu.VMEM((STEPS, ROWS, lz), f32),
                pltpu.VMEM((STEPS, ROWS, LANES), f32),
                pltpu.VMEM((STEPS, ROWS, LANES), f32),
                pltpu.VMEM((STEPS, ly, LANES), f32),
                pltpu.VMEM((3, tile, LANES), f32),
                pltpu.SMEM(permittivity.shape, f32),
                pltpu.SMEM(ports.shape, jnp.int32),
                pltpu.SMEM(amplitudes.shape, f32),
                pltpu.VMEM((ly, lx), jnp.int32),
                pltpu.SemaphoreType.DMA((10,)),
                pltpu.SemaphoreType.DMA((STEPS, 12)),
                pltpu.SemaphoreType.DMA((STEPS, 12)),
                pltpu.SemaphoreType.DMA((3,)),
                pltpu.SemaphoreType.DMA((3,)),
            ],
            compiler_params=pltpu.CompilerParams(collective_id=0, has_side_effects=True),
            name="reverse_steps",
        )(permittivity, ports, amplitudes, design_mask.T, e_adjoint, h_adjoint, snapshots, material)
        e, h, g = (pltpu.with_memory_space_constraint(v, pltpu.VMEM) for v in (e, h, g))
        e, h, g = pl.pallas_call(
            write_out,
            out_shape=(
                jax.ShapeDtypeStruct(e_adjoint.shape, f32),
                jax.ShapeDtypeStruct(h_adjoint.shape, f32),
                jax.ShapeDtypeStruct((own, lx), f32),
            ),
            in_specs=[vmem, vmem, vmem],
            out_specs=(any_spec, any_spec, vmem),
            scratch_shapes=[pltpu.SemaphoreType.DMA((2,))],
            name="write_out",
        )(e, h, g)
        return e, h, g.T

    placed = (
        P(None, "gx", "gy", "gz"),
        P(None, "gx", "gy", "gz"),
        P(None, None, "gx", "gy", "gz"),
        P("gx", "gy", "gz"),
        P(),
        P("gx", "gy"),
        P(),
        P(),
    )
    return jax.shard_map(
        body,
        mesh=mesh,
        in_specs=placed,
        out_specs=(P(None, "gx", "gy", "gz"), P(None, "gx", "gy", "gz"), P("gx", ("gy", "gz"))),
        check_vma=False,
    )
```

```python
import jax
import jax.numpy as jnp
from jax import lax
from jax.experimental import pallas as pl
from jax.experimental.pallas import tpu as pltpu
from jax.sharding import PartitionSpec as P

STEPS = 2
AXES = ("gx", "gy", "gz")
LANES = 128
ROWS = 8
half = 0.5
U_MAG, U_PRE, U_POST, U_PACK = 8, 4, 8, 8

EX, EY, EZ, PX, PY, PZ, D1, D2, D3, D4, D5, D6 = range(12)
OFFSETS = (
    (-1, 0, 0), (0, -1, 0), (0, 0, -1),
    (1, 0, 0), (0, 1, 0), (0, 0, 1),
    (1, 0, -1), (1, -1, 0), (-1, 1, 0), (0, 1, -1), (0, -1, 1), (-1, 0, 1),
)


def kernel(mesh_sizes, extent, perm_in, ports_in, amps_in, mask_in, e_in, h_in, s_in, m_in,
           e_v, h_v, g_out,
           s_v, m_v, c_v, src_v,
           x_e, y_e, z_e, x_p, y_p, z_p, y_t, y_b, rows_v, g_v,
           r_ex, r_ey, r_ez, r_px, r_py, r_pz, r_d1, r_d2, r_d3, r_d4, r_d5, r_d6, r_g,
           perm, ports, amps, mask_v, in_sem, send_sem, recv_sem, gs_sem, gr_sem):
    _, lx, ly, lz = e_in.shape
    nt = lz // LANES
    off = 2 * lx
    f32 = jnp.float32
    nmat = perm_in.shape[0]
    nport = ports_in.shape[0]
    me = tuple(lax.axis_index(a) for a in AXES)
    start = (me[0] * lx, me[1] * ly, me[2] * lz)
    nz_dev = mesh_sizes[2]

    def exists(o):
        ok = None
        for a in range(3):
            if o[a] == 0:
                continue
            c = me[a] + o[a]
            t = (c >= 0) & (c < mesh_sizes[a])
            ok = t if ok is None else ok & t
        return ok

    def at(o):
        return tuple(me[a] + o[a] for a in range(3))

    high, low_part = pl.ds(ly - ROWS, ROWS), pl.ds(0, ly - ROWS)
    load_e, load_h = [], []
    for k, d in enumerate((high, low_part)):
        load_e.append(pltpu.make_async_copy(e_in.at[:, :, d], e_v.at[:, 0:lx, d], in_sem.at[2 + 2 * k]))
        load_h.append(pltpu.make_async_copy(h_in.at[:, :, d], h_v.at[:, :, d], in_sem.at[3 + 2 * k]))
    load_m = pltpu.make_async_copy(m_in, m_v, in_sem.at[0])
    load_s = pltpu.make_async_copy(s_in, s_v, in_sem.at[1])
    load_small = [
        pltpu.make_async_copy(a, b, in_sem.at[6 + i])
        for i, (a, b) in enumerate(((perm_in, perm), (ports_in, ports), (amps_in, amps), (mask_in, mask_v)))
    ]
    for c in [load_e[0], load_h[0], load_e[1], load_h[1]] + load_small:
        c.start()

    barrier = pltpu.get_barrier_semaphore()
    count = jnp.int32(0)
    greet = list(OFFSETS)
    for d in range(2, nz_dev):
        greet += [(0, 0, d), (0, 0, -d)]
    for o in greet:
        ok = exists(o)
        count = count + ok.astype(jnp.int32)

        @pl.when(ok)
        def _(o=o):
            pl.semaphore_signal(barrier, inc=1, device_id=at(o), device_id_type=pl.DeviceIdType.MESH)

    recv = (r_ex, r_ey, r_ez, r_px, r_py, r_pz, r_d1, r_d2, r_d3, r_d4, r_d5, r_d6)

    def source(msg, phase):
        first = phase == 0
        if msg == EX:
            return e_in.at[1:3, 0] if first else x_e.at[phase, 0:2]
        if msg == EY:
            return y_e.at[phase]
        if msg == EZ:
            return z_e.at[phase]
        if msg == PX:
            return x_p.at[phase]
        if msg == PY:
            return y_p.at[phase]
        if msg == PZ:
            return z_p.at[phase]
        if msg == D1:
            return e_in.at[0, lx - 1, :, 0:LANES] if first else x_e.at[phase, 2, :, 0:LANES]
        if msg == D2:
            return e_in.at[0, lx - 1, 0:ROWS, :] if first else x_e.at[phase, 2, 0:ROWS, :]
        if msg == D3:
            return e_in.at[1, 0, ly - ROWS:ly, :] if first else x_e.at[phase, 0, ly - ROWS:ly, :]
        if msg == D4:
            return z_e.at[phase, ly - ROWS:ly, :]
        if msg == D5:
            return z_e.at[phase, 0:ROWS, :]
        return e_in.at[2, 0, :, lz - LANES:lz] if first else x_e.at[phase, 1, :, lz - LANES:lz]

    def copy(msg, phase):
        return pltpu.make_async_remote_copy(
            src_ref=source(msg, phase), dst_ref=recv[msg].at[phase],
            send_sem=send_sem.at[phase, msg], recv_sem=recv_sem.at[phase, msg],
            device_id=at(OFFSETS[msg]), device_id_type=pl.DeviceIdType.MESH)

    def send(msg, phase):
        @pl.when(exists(OFFSETS[msg]))
        def _():
            copy(msg, phase).start()

    def wait_send(msg, phase):
        @pl.when(exists(OFFSETS[msg]))
        def _():
            copy(msg, phase).wait_send()

    def comes(msg):
        return exists(tuple(-o for o in OFFSETS[msg]))

    def wait_recv(msg, phase):
        @pl.when(comes(msg))
        def _():
            copy(msg, phase).wait_recv()

    for c in (1, 2):
        e_v[c, lx] = jnp.zeros((ly, lz), f32)

    for msg in range(12):
        @pl.when(jnp.logical_not(comes(msg)))
        def _(msg=msg):
            recv[msg][...] = jnp.zeros(recv[msg].shape, f32)

    row = lax.broadcasted_iota(jnp.int32, (ly, lz), 0)
    lane = lax.broadcasted_iota(jnp.int32, (ly, lz), 1)
    row1 = lax.broadcasted_iota(jnp.int32, (ly, LANES), 0)
    lane1 = lax.broadcasted_iota(jnp.int32, (ly, LANES), 1)
    row8 = lax.broadcasted_iota(jnp.int32, (ROWS, LANES), 0)
    zero1 = jnp.zeros((ly, LANES), f32)

    def wide(t):
        return t[0] if nt == 1 else jnp.concatenate([t[k] for k in range(nt)], 1)

    def up(v, axis):
        n = v.shape[axis]
        i = lax.broadcasted_iota(jnp.int32, v.shape, axis)
        return jnp.where(i == n - 1, 0.0, pltpu.roll(v, n - 1, axis))

    def down(v, axis):
        i = lax.broadcasted_iota(jnp.int32, v.shape, axis)
        return jnp.where(i == 0, 0.0, pltpu.roll(v, 1, axis))

    def pick(tile, from_lane, to, acc):
        shift = lax.rem(to + (LANES - from_lane), LANES)
        return jnp.where(lane1 == to, pltpu.roll(tile, shift, 1), acc)

    def put(dst, i, x, v, r):
        for k in range(nt):
            dst[i, k, pl.ds(x, 1), :] = v[r:r + 1, k * LANES:(k + 1) * LANES]

    def put_wide(dst, i, v):
        for k in range(nt):
            dst[i, k] = v[:, k * LANES:(k + 1) * LANES]

    def pick_e(x, ex, ey, ez, acc):
        acc = pick(ex[:, 0:LANES], 0, 2 * x, acc)
        acc = pick(ey[:, 0:LANES], 0, off + 2 * x, acc)
        return pick(ez[:, lz - LANES:lz], LANES - 1, 2 * x + 1, acc)

    def top_y(phase, ex, ey, ez, hx, hz):
        put_wide(y_p.at[phase], 0, hx + half * (ez + (up(ey, 1) - ey)))
        put_wide(y_p.at[phase], 1, hz - half * ((up(ey, 0) - ey) + ex))

    def top_x(phase):
        ex, ey, ez = e_v[0, lx - 1], e_v[1, lx - 1], e_v[2, lx - 1]
        x_p[phase, 0] = h_v[1, lx - 1] - half * ((up(ex, 1) - ex) + ez)
        x_p[phase, 1] = h_v[2, lx - 1] + half * (ey + (up(ex, 0) - ex))

    def magnetic(phase):
        def one(x, acc):
            ex, ey, ez = e_v[0, x], e_v[1, x], e_v[2, x]
            dey, dez = e_v[1, x + 1] - ey, e_v[2, x + 1] - ez
            hx = h_v[0, x] - half * ((up(ez, 0) - ez) - (up(ey, 1) - ey))
            hy = h_v[1, x] - half * ((up(ex, 1) - ex) - dez)
            hz = h_v[2, x] - half * (dey - (up(ex, 0) - ex))
            h_v[0, x] = hx
            h_v[1, x] = hy
            h_v[2, x] = hz
            acc = pick(hy[:, lz - LANES:lz], LANES - 1, 2 * x + 1, acc)
            return pick(hx[:, lz - LANES:lz], LANES - 1, off + 2 * x + 1, acc)

        z_p[phase] = lax.fori_loop(0, lx, one, zero1, unroll=U_MAG)

    def save_e(phase):
        x_e[phase, 0] = e_v[1, 0]
        x_e[phase, 1] = e_v[2, 0]
        x_e[phase, 2] = e_v[0, lx - 1]

    def pre(step):
        def one(x, carry):
            hy_b, hz_b, acc_c, acc_l, acc_g = carry
            ex, ey, ez = e_v[0, x], e_v[1, x], e_v[2, x]
            hx, hy, hz = h_v[0, x], h_v[1, x], h_v[2, x]
            if step == 0:
                mat = m_v[x]
                c = coefs[0]
                for k in range(1, nmat):
                    c = jnp.where(mat == k, coefs[k], c)
                c_v[x] = c
            else:
                c = c_v[x]
                total, change = None, []
                for comp, val in enumerate((ex, ey, ez)):
                    mid = s_v[step, comp, x].astype(f32)
                    t = val * (s_v[step - 1, comp, x].astype(f32) - mid)
                    total = t if total is None else total + t
                    change.append(mid - s_v[step + 1, comp, x].astype(f32))
            ex = ex + c * ((hz - down(hz, 0)) - (hy - down(hy, 1)))
            ey = ey + c * ((hx - down(hx, 1)) - (hz - hz_b))
            ez = ez + c * ((hy - hy_b) - (hx - down(hx, 0)))
            for p in range(nport):
                ez = ez + src_v[step, jnp.where(port_x[p] == x, p, nport)]
            e_v[0, x] = ex
            e_v[1, x] = ey
            e_v[2, x] = ez
            if step == 0:
                for i, (v, r) in enumerate(((ex, 0), (ez, 0), (ex, -1), (ey, -1), (ez, -1), (hx, -1), (hz, -1), (c, 0), (c, -1))):
                    put(y_b, i, x, v, r % ly)
            else:
                for val, d in zip((ex, ey, ez), change):
                    total = total + val * d
                fold = total[:, 0:LANES]
                for k in range(1, nt):
                    fold = fold + total[:, k * LANES:(k + 1) * LANES]
                acc_g = jnp.where(lane1 == 2 * x, jnp.sum(fold, axis=1, keepdims=True), acc_g)
                wx, wy, wz = (c * d for d in change)
                for i, (v, r) in enumerate(((wx, 0), (wz, 0), (wx, -1), (wy, -1), (wz, -1))):
                    put(y_b, i, x, v, r % ly)
                acc_c = pick(wx[:, 0:LANES], 0, 2 * x + 1, acc_c)
                acc_c = pick(wy[:, 0:LANES], 0, off + 2 * x + 1, acc_c)
                acc_c = pick(wx[:, lz - LANES:lz], LANES - 1, 2 * x, acc_c)
                acc_c = pick(wy[:, lz - LANES:lz], LANES - 1, off + 2 * x, acc_c)
                acc_l = pick(wz[:, lz - LANES:lz], LANES - 1, 2 * x, acc_l)
            return hy, hz, acc_c, acc_l, acc_g

        zero = jnp.zeros((ly, lz), f32)
        return lax.fori_loop(0, lx, one, (zero, zero, zero1, zero1, zero1), unroll=U_PRE)[2:]

    flags = tuple((me[a] > 0).astype(f32) for a in range(3))

    def pad_high(t):
        return jnp.concatenate([jnp.zeros((ly, lz - LANES), f32), t], 1) if lz > LANES else t

    def halos(phase):
        fx, fy, fz = flags
        d1 = pad_high(pltpu.roll(r_d1[phase], LANES - 1, 1))
        hy_x = (r_px[phase, 0] + half * x_e[phase, 1]) * fx - jnp.where(lane == lz - 1, half * d1, 0.0)
        d2 = jnp.broadcast_to(r_d2[phase, 0:1, :], (ly, lz))
        hz_x = (r_px[phase, 1] - half * x_e[phase, 0]) * fx + jnp.where(row == ly - 1, half * d2, 0.0)
        c0, c1 = c_v[0], c_v[lx - 1]
        dhy = half * r_ex[phase, 1]
        dhz = -half * r_ex[phase, 0]
        h_v[1, lx - 1] = h_v[1, lx - 1] + dhy
        h_v[2, lx - 1] = h_v[2, lx - 1] + dhz
        planes = (
            (1, 0, c0 * hz_x), (2, 0, -c0 * hy_x),
            (0, lx - 1, c1 * ((dhz - down(dhz, 0)) - (dhy - down(dhy, 1)))),
            (1, lx - 1, -c1 * dhz), (2, lx - 1, c1 * dhy),
        )
        for comp, x, d in planes:
            e_v[comp, x] = e_v[comp, x] + d
        rx = lax.broadcasted_iota(jnp.int32, (lx, LANES), 0)
        cx = lax.broadcasted_iota(jnp.int32, (lx, LANES), 1)
        d4 = jnp.broadcast_to(r_d4[phase, ROWS - 1:ROWS, :], (lx, LANES))
        d4 = jnp.sum(jnp.where(cx == off + 2 * rx, d4, 0.0), axis=1, keepdims=True)
        ry = lax.broadcasted_iota(jnp.int32, (lx, lz), 0)
        cy = lax.broadcasted_iota(jnp.int32, (lx, lz), 1)
        hx_y = (wide(r_py[phase, 0]) - half * wide(y_e[phase, 1])) * fy + jnp.where(cy == lz - 1, half * d4, 0.0)
        d3 = jnp.broadcast_to(r_d3[phase, ROWS - 1:ROWS, :], (lx, lz))
        hz_y = (wide(r_py[phase, 1]) + half * wide(y_e[phase, 0])) * fy - jnp.where(ry == lx - 1, half * d3, 0.0)
        dhx = -half * wide(r_ey[phase, 1])
        dhz = half * wide(r_ey[phase, 0])
        values = (-hz_y, hx_y, dhz, (dhx - down(dhx, 1)) - (dhz - down(dhz, 0)), -dhx)
        for i, v in enumerate(values):
            put_wide(rows_v, i, v)
        own = pltpu.roll(z_e[phase], 1, 1)
        low = lane1 < off
        zh = (r_pz[phase] + jnp.where(low, -half * own, half * own)) * fz
        d5 = jnp.broadcast_to(pltpu.roll(r_d5[phase], off, 1)[0:1, :], (ly, LANES))
        zh = zh - jnp.where((row1 == ly - 1) & (lane1 >= off), half * d5, 0.0)
        d6 = pltpu.roll(r_d6[phase], off, 1)
        zh = zh + jnp.where(lane1 == off - 1, half * d6, 0.0)
        ze = half * r_ez[phase]
        odd = lax.rem(lane1, 2) == 1
        cols = jnp.where(odd, jnp.where(low, zh, -zh), ze)
        dhy = jnp.where(odd | (lane1 >= off), 0.0, -ze)
        dhx = jnp.where(odd | (lane1 >= off), 0.0, pltpu.roll(ze, LANES - off, 1))
        shift_x = jnp.where(lane1 < 2, 0.0, pltpu.roll(dhy, 2, 1))
        last = (dhy - shift_x) - (dhx - down(dhx, 0))
        return planes, values, cols, last

    rx1 = lax.broadcasted_iota(jnp.int32, (lx, LANES), 0)
    cx1 = lax.broadcasted_iota(jnp.int32, (lx, LANES), 1)
    cyw = lax.broadcasted_iota(jnp.int32, (lx, lz), 1)

    def first_rows(values, cols, last):
        for x in (0, lx - 1):
            for i, (src, comp, r) in enumerate((
                (e_v, 0, 0), (e_v, 2, 0), (e_v, 0, -1), (e_v, 1, -1), (e_v, 2, -1), (h_v, 0, -1), (h_v, 2, -1))):
                put(y_b, i, x, src[comp, x], r % ly)

        def edge(col, y, at_lane, to):
            t = jnp.where(cx1 == 2 * rx1 + at_lane, jnp.broadcast_to(col[y:y + 1], (lx, LANES)), 0.0)
            return jnp.where(cyw == to, jnp.sum(t, axis=1, keepdims=True), 0.0)

        b = [wide(y_b[i]) for i in range(9)]
        y, end = ly - 1, lz - 1
        hx_edge = edge(cols, y, off, end)
        put_wide(y_e.at[1], 0, b[0] + b[7] * (values[0] + edge(cols, 0, 1, 0) + edge(cols, 0, 0, end)))
        put_wide(y_e.at[1], 1, b[1] + b[7] * (values[1] + edge(last, 0, 0, end)))
        ex = b[2] + b[8] * (values[2] + edge(cols, y, 1, 0) + edge(cols, y, 0, end))
        ey = b[3] + b[8] * (values[3] + edge(cols, y, off + 1, 0) + hx_edge)
        ez = b[4] + b[8] * (values[4] + edge(last, y, 0, end))
        top_y(1, ex, ey, ez, b[5] - values[4] + hx_edge, b[6] + values[2])

    def gradient_part(planes, values, cols, last, acc_c, acc_l, acc_g):
        w = [wide(y_b[i]) for i in range(5)]
        total = acc_g
        for y, t in ((0, values[0] * w[0] + values[1] * w[1]), (ly - 1, values[2] * w[2] + values[3] * w[3] + values[4] * w[4])):
            t = jnp.sum(t, axis=1, keepdims=True)
            t = jnp.sum(jnp.where(cx1 == 2 * rx1, t, 0.0), axis=0, keepdims=True)
            total = total + jnp.where(row1 == y, t, 0.0)
        p = cols * acc_c
        q = p + pltpu.roll(p, LANES - 1, 1)
        q = q + pltpu.roll(q, LANES - off, 1) + last * acc_l
        total = total + jnp.where((lane1 < off) & (lax.rem(lane1, 2) == 0), q, 0.0)
        for x in (0, lx - 1):
            t = None
            for comp, at_x, d in planes:
                if at_x == x:
                    change = s_v[STEPS - 1, comp, x].astype(f32) - s_v[STEPS, comp, x].astype(f32)
                    t = d * change if t is None else t + d * change
            total = total + jnp.where(lane1 == 2 * x, jnp.sum(t, axis=1, keepdims=True), 0.0)
        return total

    top, bottom = row8 == 0, row8 == ROWS - 1
    lane8 = lax.broadcasted_iota(jnp.int32, (ROWS, LANES), 1)
    first_lane, last_lane = lane8 == 0, lane8 == LANES - 1
    nr = ly // ROWS

    def post(step, cols, last):
        def one(x, acc):
            low_col = pltpu.roll(cols, lax.rem(2 * LANES - (2 * x + 1), LANES), 1)
            high_col = pltpu.roll(cols, lax.rem(2 * LANES - (off + 2 * x + 1), LANES), 1)
            last_col = pltpu.roll(last, lax.rem(2 * LANES - (2 * x + 1), LANES), 1)
            def delta(r, k, col0, col1, row0, row1_):
                terms = []
                cut = slice(r * ROWS, (r + 1) * ROWS)
                if col0 is not None and k == 0:
                    terms.append(jnp.where(first_lane, col0[cut], 0.0))
                if col1 is not None and k == nt - 1:
                    terms.append(jnp.where(last_lane, col1[cut], 0.0))
                if row0 is not None and r == 0:
                    t = jnp.broadcast_to(rows_v[row0, k, pl.ds(x, 1), :], (ROWS, LANES))
                    terms.append(jnp.where(top, t, 0.0))
                if row1_ is not None and r == nr - 1:
                    t = jnp.broadcast_to(rows_v[row1_, k, pl.ds(x, 1), :], (ROWS, LANES))
                    terms.append(jnp.where(bottom, t, 0.0))
                return sum(terms[1:], terms[0]) if terms else None

            new = []
            for comp, args in enumerate(((low_col, low_col, 0, 2), (high_col, high_col, None, 3), (None, last_col, 1, 4))):
                strips = []
                for k in range(nt):
                    strip = []
                    for r in range(nr):
                        at_ = (comp, x, pl.ds(r * ROWS, ROWS), pl.ds(k * LANES, LANES))
                        d = delta(r, k, *args)
                        v = e_v[at_]
                        if d is not None:
                            v = v + c_v[x, r * ROWS:(r + 1) * ROWS, k * LANES:(k + 1) * LANES] * d
                            e_v[at_] = v
                        strip.append(v)
                    strips.append(jnp.concatenate(strip, 0) if nr > 1 else strip[0])
                new.append(strips)
            for comp, args in enumerate((
                ((None, high_col, None, None, 1), (None, None, None, 4, -1)),
                ((None, low_col, None, None, -1),),
                ((None, None, None, 2, 1),),
            )):
                for r in range(nr):
                    for k in range(nt):
                        at_ = (comp, x, pl.ds(r * ROWS, ROWS), pl.ds(k * LANES, LANES))
                        v = None
                        for *which, sign in args:
                            d = delta(r, k, *which)
                            if d is not None:
                                v = h_v[at_] if v is None else v
                                v = v + d if sign > 0 else v - d
                        if v is not None:
                            h_v[at_] = v
            return pick_e(x, *(wide(n) for n in new), acc) if step + 1 < STEPS else acc

        return lax.fori_loop(0, lx, one, zero1, unroll=U_POST)

    pl.semaphore_wait(barrier, count)
    for msg in (D2, D3, D1, D6, EX):
        send(msg, 0)

    def first_top(x, carry):
        for i, (src, comp) in enumerate(((e_v, 0), (e_v, 1), (e_v, 2), (h_v, 0), (h_v, 2))):
            put(y_t, i, x, src[comp, x, ly - ROWS:ly, :], ROWS - 1)
        return carry

    def first_pack(x, acc):
        ex, ey, ez = e_v[0, x], e_v[1, x], e_v[2, x]
        put(y_e.at[0], 0, x, ex, 0)
        put(y_e.at[0], 1, x, ez, 0)
        return pick_e(x, ex, ey, ez, acc)

    load_e[0].wait()
    load_h[0].wait()
    lax.fori_loop(0, lx, first_top, 0, unroll=U_PACK)
    top_y(0, *(wide(y_t[i]) for i in range(5)))
    send(PY, 0)
    load_e[1].wait()
    load_m.start()
    load_s.start()
    z_e[0] = lax.fori_loop(0, lx, first_pack, zero1, unroll=U_PACK)
    for msg in (EY, D4, D5, EZ):
        send(msg, 0)
    load_h[1].wait()
    top_x(0)
    send(PX, 0)
    magnetic(0)
    send(PZ, 0)
    save_e(0)

    for c in load_small:
        c.wait()
    plane = extent[1] * extent[2]
    port_x = []
    for p in range(nport):
        cell = ports[p]
        px = lax.div(cell, plane)
        rest = lax.rem(cell, plane)
        py = lax.div(rest, extent[2]) - start[1]
        pz = lax.rem(rest, extent[2]) - start[2]
        port_x.append(px - start[0])
        hit = (row == py) & (lane == pz)
        for s in range(STEPS):
            src_v[s, p] = jnp.where(hit, amps[s, p], 0.0)
    for s in range(STEPS):
        src_v[s, nport] = jnp.zeros((ly, lz), f32)
    coefs = [half / jnp.full((ly, lz), perm[k], f32) for k in range(nmat)]
    load_m.wait()
    pre(0)
    for msg in range(12):
        wait_recv(msg, 0)
    planes, values, cols, last = halos(0)
    first_rows(values, cols, last)
    for msg in (EY, PY):
        send(msg, 1)
    z_e[1] = post(0, cols, last)
    save_e(1)
    for msg in (D2, D3, D1, D6, D4, D5, EX):
        send(msg, 1)
    top_x(1)
    for msg in (PX, EZ):
        send(msg, 1)
    magnetic(1)
    send(PZ, 1)
    load_s.wait()
    weights = pre(1)
    spread = lax.broadcasted_iota(jnp.int32, (lx, LANES), 1) == 2 * lax.broadcasted_iota(jnp.int32, (lx, LANES), 0)
    mask = jnp.dot(mask_v[...].astype(f32), spread.astype(f32), preferred_element_type=f32)
    for msg in range(12):
        wait_recv(msg, 1)
    planes, values, cols, last = halos(1)
    acc = gradient_part(planes, values, cols, last, *weights)

    own_rows = ly // nz_dev
    tile = g_out.shape[0]
    g_v[...] = acc * mask

    def tile_of(k):
        return pl.ds(pl.multiple_of((k * own_rows) // tile * tile, ROWS), tile)

    gcopies = []
    for d in range(1, nz_dev):
        peer = lax.rem(me[2] + d, nz_dev)
        gcopies.append(pltpu.make_async_remote_copy(
            src_ref=g_v.at[tile_of(peer)], dst_ref=r_g.at[d - 1],
            send_sem=gs_sem.at[d - 1], recv_sem=gr_sem.at[d - 1],
            device_id=(me[0], me[1], peer), device_id_type=pl.DeviceIdType.MESH))
    for c in gcopies:
        c.start()
    post(1, cols, last)
    for phase in range(STEPS):
        for msg in range(12):
            wait_send(msg, phase)
    total = g_v[tile_of(me[2])]
    for d, c in enumerate(gcopies):
        c.wait_recv()
        total = total + r_g[d]
    shift = lax.rem(tile - lax.rem(me[2] * own_rows, tile), tile)
    g_out[...] = pltpu.roll(total, shift, 0)
    for c in gcopies:
        c.wait_send()


def write_out(e_v, h_v, g_v, e_out, h_out, g_out, sem):
    lx = h_v.shape[1]
    outs = [
        pltpu.make_async_copy(e_v.at[:, 0:lx], e_out, sem.at[0]),
        pltpu.make_async_copy(h_v, h_out, sem.at[1]),
    ]
    for c in outs:
        c.start()
    own, _ = g_out.shape
    pick = lax.broadcasted_iota(jnp.int32, (LANES, LANES), 0) == 2 * lax.broadcasted_iota(jnp.int32, (LANES, LANES), 1)
    g = jnp.dot(g_v[...], pick.astype(jnp.float32), precision=lax.Precision.HIGHEST, preferred_element_type=jnp.float32)
    g_out[...] = g[0:own, 0:lx]
    for c in outs:
        c.wait()


def solution(mesh):
    mesh_sizes = tuple(mesh.shape[a] for a in AXES)

    def body(e_adjoint, h_adjoint, snapshots, material, permittivity, design_mask, ports, amplitudes):
        _, lx, ly, lz = e_adjoint.shape
        extent = (lx * mesh_sizes[0], ly * mesh_sizes[1], lz * mesh_sizes[2])
        nport = ports.shape[0]
        nt = lz // LANES
        f32 = jnp.float32
        own = ly // mesh_sizes[2]
        tile = max(ROWS, own)
        any_spec = pl.BlockSpec(memory_space=pl.ANY)
        vmem = pl.BlockSpec(memory_space=pltpu.VMEM)
        e, h, g = pl.pallas_call(
            lambda *refs: kernel(mesh_sizes, extent, *refs),
            out_shape=(
                pltpu.VMEM((3, lx + 1, ly, lz), f32),
                pltpu.VMEM((3, lx, ly, lz), f32),
                pltpu.VMEM((tile, LANES), f32),
            ),
            in_specs=[any_spec, any_spec, any_spec, any_spec, any_spec, any_spec, any_spec, any_spec],
            out_specs=(vmem, vmem, vmem),
            scratch_shapes=[
                pltpu.VMEM(snapshots.shape, snapshots.dtype),
                pltpu.VMEM((lx, ly, lz), jnp.int32),
                pltpu.VMEM((lx, ly, lz), f32),
                pltpu.VMEM((STEPS, nport + 1, ly, lz), f32),
                pltpu.VMEM((STEPS, 3, ly, lz), f32),
                pltpu.VMEM((STEPS, 2, nt, lx, LANES), f32),
                pltpu.VMEM((STEPS, ly, LANES), f32),
                pltpu.VMEM((STEPS, 2, ly, lz), f32),
                pltpu.VMEM((STEPS, 2, nt, lx, LANES), f32),
                pltpu.VMEM((STEPS, ly, LANES), f32),
                pltpu.VMEM((5, nt, lx, LANES), f32),
                pltpu.VMEM((9, nt, lx, LANES), f32),
                pltpu.VMEM((5, nt, lx, LANES), f32),
                pltpu.VMEM((ly, LANES), f32),
                pltpu.VMEM((STEPS, 2, ly, lz), f32),
                pltpu.VMEM((STEPS, 2, nt, lx, LANES), f32),
                pltpu.VMEM((STEPS, ly, LANES), f32),
                pltpu.VMEM((STEPS, 2, ly, lz), f32),
                pltpu.VMEM((STEPS, 2, nt, lx, LANES), f32),
                pltpu.VMEM((STEPS, ly, LANES), f32),
                pltpu.VMEM((STEPS, ly, LANES), f32),
                pltpu.VMEM((STEPS, ROWS, lz), f32),
                pltpu.VMEM((STEPS, ROWS, lz), f32),
                pltpu.VMEM((STEPS, ROWS, LANES), f32),
                pltpu.VMEM((STEPS, ROWS, LANES), f32),
                pltpu.VMEM((STEPS, ly, LANES), f32),
                pltpu.VMEM((3, tile, LANES), f32),
                pltpu.SMEM(permittivity.shape, f32),
                pltpu.SMEM(ports.shape, jnp.int32),
                pltpu.SMEM(amplitudes.shape, f32),
                pltpu.VMEM((ly, lx), jnp.int32),
                pltpu.SemaphoreType.DMA((10,)),
                pltpu.SemaphoreType.DMA((STEPS, 12)),
                pltpu.SemaphoreType.DMA((STEPS, 12)),
                pltpu.SemaphoreType.DMA((3,)),
                pltpu.SemaphoreType.DMA((3,)),
            ],
            compiler_params=pltpu.CompilerParams(collective_id=0, has_side_effects=True),
            name="reverse_steps",
        )(permittivity, ports, amplitudes, design_mask.T, e_adjoint, h_adjoint, snapshots, material)
        e, h, g = (pltpu.with_memory_space_constraint(v, pltpu.VMEM) for v in (e, h, g))
        e, h, g = pl.pallas_call(
            write_out,
            out_shape=(
                jax.ShapeDtypeStruct(e_adjoint.shape, f32),
                jax.ShapeDtypeStruct(h_adjoint.shape, f32),
                jax.ShapeDtypeStruct((own, lx), f32),
            ),
            in_specs=[vmem, vmem, vmem],
            out_specs=(any_spec, any_spec, vmem),
            scratch_shapes=[pltpu.SemaphoreType.DMA((2,))],
            name="write_out",
        )(e, h, g)
        return e, h, g.T

    placed = (
        P(None, "gx", "gy", "gz"),
        P(None, "gx", "gy", "gz"),
        P(None, None, "gx", "gy", "gz"),
        P("gx", "gy", "gz"),
        P(),
        P("gx", "gy"),
        P(),
        P(),
    )
    return jax.shard_map(
        body,
        mesh=mesh,
        in_specs=placed,
        out_specs=(P(None, "gx", "gy", "gz"), P(None, "gx", "gy", "gz"), P("gx", ("gy", "gz"))),
        check_vma=False,
    )
```

```python
import jax
import jax.numpy as jnp
from jax import lax
from jax.experimental import pallas as pl
from jax.experimental.pallas import tpu as pltpu
from jax.sharding import PartitionSpec as P

STEPS = 2
AXES = ("gx", "gy", "gz")
LANES = 128
ROWS = 8
half = 0.5
U_MAG, U_PRE, U_POST, U_PACK, U_INNER = 8, 4, 8, 8, 6

EX, EY, EZ, PX, PY, PZ, D1, D2, D3, D4, D5, D6 = range(12)
OFFSETS = (
    (-1, 0, 0), (0, -1, 0), (0, 0, -1),
    (1, 0, 0), (0, 1, 0), (0, 0, 1),
    (1, 0, -1), (1, -1, 0), (-1, 1, 0), (0, 1, -1), (0, -1, 1), (-1, 0, 1),
)


def rem(a, b):
    return a % b if isinstance(a, int) else lax.rem(a, b)


def kernel(mesh_sizes, extent, perm_in, ports_in, amps_in, mask_in, e_in, h_in, s_in, m_in,
           e_v, h_v, g_out,
           s_v, m_v, c_v, src_v,
           x_e, y_e, z_e, x_p, y_p, z_p, y_t, y_b, d_r, d_s, rows_v, g_v,
           r_ex, r_ey, r_ez, r_px, r_py, r_pz, r_d1, r_d2, r_d3, r_d4, r_d5, r_d6, r_g,
           perm, ports, amps, mask_v, in_sem, send_sem, recv_sem, gs_sem, gr_sem):
    _, lx, ly, lz = e_in.shape
    nt = lz // LANES
    off = 2 * lx
    f32 = jnp.float32
    nmat = perm_in.shape[0]
    nport = ports_in.shape[0]
    me = tuple(lax.axis_index(a) for a in AXES)
    start = (me[0] * lx, me[1] * ly, me[2] * lz)
    nz_dev = mesh_sizes[2]

    def exists(o):
        ok = None
        for a in range(3):
            if o[a] == 0:
                continue
            c = me[a] + o[a]
            t = (c >= 0) & (c < mesh_sizes[a])
            ok = t if ok is None else ok & t
        return ok

    def at(o):
        return tuple(me[a] + o[a] for a in range(3))

    high, low_part = pl.ds(ly - ROWS, ROWS), pl.ds(0, ly - ROWS)
    load_e, load_h = [], []
    for k, d in enumerate((high, low_part)):
        load_e.append(pltpu.make_async_copy(e_in.at[:, :, d], e_v.at[:, 0:lx, d], in_sem.at[2 + 2 * k]))
        load_h.append(pltpu.make_async_copy(h_in.at[:, :, d], h_v.at[:, :, d], in_sem.at[3 + 2 * k]))
    load_m = pltpu.make_async_copy(m_in, m_v, in_sem.at[0])
    load_s = pltpu.make_async_copy(s_in, s_v, in_sem.at[1])
    load_small = [
        pltpu.make_async_copy(a, b, in_sem.at[6 + i])
        for i, (a, b) in enumerate(((perm_in, perm), (ports_in, ports), (amps_in, amps), (mask_in, mask_v)))
    ]
    for c in [load_e[0], load_h[0], load_e[1], load_h[1]] + load_small:
        c.start()

    barrier = pltpu.get_barrier_semaphore()
    count = jnp.int32(0)
    greet = list(OFFSETS)
    for d in range(2, nz_dev):
        greet += [(0, 0, d), (0, 0, -d)]
    for o in greet:
        ok = exists(o)
        count = count + ok.astype(jnp.int32)

        @pl.when(ok)
        def _(o=o):
            pl.semaphore_signal(barrier, inc=1, device_id=at(o), device_id_type=pl.DeviceIdType.MESH)

    recv = (r_ex, r_ey, r_ez, r_px, r_py, r_pz, r_d1, r_d2, r_d3, r_d4, r_d5, r_d6)

    def source(msg, phase):
        first = phase == 0
        if msg == EX:
            return e_in.at[1:3, 0] if first else x_e.at[phase, 0:2]
        if msg == EY:
            return y_e.at[phase]
        if msg == EZ:
            return z_e.at[phase]
        if msg == PX:
            return x_p.at[phase]
        if msg == PY:
            return y_p.at[phase]
        if msg == PZ:
            return z_p.at[phase]
        if msg == D1:
            return e_in.at[0, lx - 1, :, 0:LANES] if first else x_e.at[phase, 2, :, 0:LANES]
        if msg == D2:
            return e_in.at[0, lx - 1, 0:ROWS, :] if first else d_r.at[0]
        if msg == D3:
            return e_in.at[1, 0, ly - ROWS:ly, :] if first else d_r.at[1]
        if msg == D4:
            return d_s.at[phase, 0]
        if msg == D5:
            return d_s.at[phase, 1]
        return e_in.at[2, 0, :, lz - LANES:lz] if first else x_e.at[phase, 1, :, lz - LANES:lz]

    def copy(msg, phase):
        return pltpu.make_async_remote_copy(
            src_ref=source(msg, phase), dst_ref=recv[msg].at[phase],
            send_sem=send_sem.at[phase, msg], recv_sem=recv_sem.at[phase, msg],
            device_id=at(OFFSETS[msg]), device_id_type=pl.DeviceIdType.MESH)

    def send(msg, phase):
        @pl.when(exists(OFFSETS[msg]))
        def _():
            copy(msg, phase).start()

    def wait_send(msg, phase):
        @pl.when(exists(OFFSETS[msg]))
        def _():
            copy(msg, phase).wait_send()

    def comes(msg):
        return exists(tuple(-o for o in OFFSETS[msg]))

    def wait_recv(msg, phase):
        @pl.when(comes(msg))
        def _():
            copy(msg, phase).wait_recv()

    for c in (1, 2):
        e_v[c, lx] = jnp.zeros((ly, lz), f32)

    for msg in range(12):
        @pl.when(jnp.logical_not(comes(msg)))
        def _(msg=msg):
            recv[msg][...] = jnp.zeros(recv[msg].shape, f32)

    row = lax.broadcasted_iota(jnp.int32, (ly, lz), 0)
    lane = lax.broadcasted_iota(jnp.int32, (ly, lz), 1)
    row1 = lax.broadcasted_iota(jnp.int32, (ly, LANES), 0)
    lane1 = lax.broadcasted_iota(jnp.int32, (ly, LANES), 1)
    row8 = lax.broadcasted_iota(jnp.int32, (ROWS, LANES), 0)
    zero1 = jnp.zeros((ly, LANES), f32)

    def wide(t):
        return t[0] if nt == 1 else jnp.concatenate([t[k] for k in range(nt)], 1)

    def up(v, axis):
        n = v.shape[axis]
        i = lax.broadcasted_iota(jnp.int32, v.shape, axis)
        return jnp.where(i == n - 1, 0.0, pltpu.roll(v, n - 1, axis))

    def down(v, axis):
        i = lax.broadcasted_iota(jnp.int32, v.shape, axis)
        return jnp.where(i == 0, 0.0, pltpu.roll(v, 1, axis))

    def pick(tile, from_lane, to, acc):
        shift = rem(to + (LANES - from_lane), LANES)
        return jnp.where(lane1 == to, pltpu.roll(tile, shift, 1), acc)

    def put(dst, i, x, v, r):
        for k in range(nt):
            dst[i, k, pl.ds(x, 1), :] = v[r:r + 1, k * LANES:(k + 1) * LANES]

    def put_wide(dst, i, v):
        for k in range(nt):
            dst[i, k] = v[:, k * LANES:(k + 1) * LANES]

    def pick_e(x, ex, ey, acc):
        acc = pick(ex[:, 0:LANES], 0, 2 * x, acc)
        return pick(ey[:, 0:LANES], 0, off + 2 * x, acc)

    rx1 = lax.broadcasted_iota(jnp.int32, (lx, LANES), 0)
    cx1 = lax.broadcasted_iota(jnp.int32, (lx, LANES), 1)

    def lines(phase, ey, ez):
        for i, (t, at_lane) in enumerate(((ey[:, 0:1], off), (ez[:, lz - 1:lz], 1))):
            t = jnp.sum(jnp.where(cx1 == 2 * rx1 + at_lane, t, 0.0), axis=0, keepdims=True)
            d_s[phase, i] = jnp.broadcast_to(t, (ROWS, LANES))

    def top_y(phase, ex, ey, ez, hx, hz):
        put_wide(y_p.at[phase], 0, hx + half * (ez + (up(ey, 1) - ey)))
        put_wide(y_p.at[phase], 1, hz - half * ((up(ey, 0) - ey) + ex))

    def top_x(phase, ex, ey, ez, hy, hz):
        x_p[phase, 0] = hy - half * ((up(ex, 1) - ex) + ez)
        x_p[phase, 1] = hz + half * (ey + (up(ex, 0) - ex))

    def magnetic(phase):
        def one(x, acc):
            ex, ey, ez = e_v[0, x], e_v[1, x], e_v[2, x]
            dey, dez = e_v[1, x + 1] - ey, e_v[2, x + 1] - ez
            hx = h_v[0, x] - half * ((up(ez, 0) - ez) - (up(ey, 1) - ey))
            hy = h_v[1, x] - half * ((up(ex, 1) - ex) - dez)
            hz = h_v[2, x] - half * (dey - (up(ex, 0) - ex))
            h_v[0, x] = hx
            h_v[1, x] = hy
            h_v[2, x] = hz
            acc = pick(hy[:, lz - LANES:lz], LANES - 1, 2 * x + 1, acc)
            return pick(hx[:, lz - LANES:lz], LANES - 1, off + 2 * x + 1, acc)

        z_p[phase] = lax.fori_loop(0, lx, one, zero1, unroll=U_MAG)

    def save_e(phase):
        x_e[phase, 0] = e_v[1, 0]
        x_e[phase, 1] = e_v[2, 0]
        x_e[phase, 2] = e_v[0, lx - 1]

    def pre(step):
        def one(x, carry):
            hy_b, hz_b, acc_c, acc_l, acc_g = carry
            ex, ey, ez = e_v[0, x], e_v[1, x], e_v[2, x]
            hx, hy, hz = h_v[0, x], h_v[1, x], h_v[2, x]
            if step == 0:
                mat = m_v[x]
                c = coefs[0]
                for k in range(1, nmat):
                    c = jnp.where(mat == k, coefs[k], c)
                c_v[x] = c
            else:
                c = c_v[x]
                total, change = None, []
                for comp, val in enumerate((ex, ey, ez)):
                    mid = s_v[step, comp, x].astype(f32)
                    t = val * (s_v[step - 1, comp, x].astype(f32) - mid)
                    total = t if total is None else total + t
                    change.append(mid - s_v[step + 1, comp, x].astype(f32))
            ex = ex + c * ((hz - down(hz, 0)) - (hy - down(hy, 1)))
            ey = ey + c * ((hx - down(hx, 1)) - (hz - hz_b))
            ez = ez + c * ((hy - hy_b) - (hx - down(hx, 0)))
            for p in range(nport):
                ez = ez + src_v[step, jnp.where(port_x[p] == x, p, nport)]
            e_v[0, x] = ex
            e_v[1, x] = ey
            e_v[2, x] = ez
            if step == 0:
                for i, (v, r) in enumerate(((ex, 0), (ez, 0), (ex, -1), (ey, -1), (ez, -1), (hx, -1), (hz, -1), (c, 0), (c, -1))):
                    put(y_b, i, x, v, r % ly)
            else:
                for val, d in zip((ex, ey, ez), change):
                    total = total + val * d
                fold = total[:, 0:LANES]
                for k in range(1, nt):
                    fold = fold + total[:, k * LANES:(k + 1) * LANES]
                acc_g = jnp.where(lane1 == 2 * x, jnp.sum(fold, axis=1, keepdims=True), acc_g)
                wx, wy, wz = (c * d for d in change)
                for i, (v, r) in enumerate(((wx, 0), (wz, 0), (wx, -1), (wy, -1), (wz, -1))):
                    put(y_b, i, x, v, r % ly)
                acc_c = pick(wx[:, 0:LANES], 0, 2 * x + 1, acc_c)
                acc_c = pick(wy[:, 0:LANES], 0, off + 2 * x + 1, acc_c)
                acc_c = pick(wx[:, lz - LANES:lz], LANES - 1, 2 * x, acc_c)
                acc_c = pick(wy[:, lz - LANES:lz], LANES - 1, off + 2 * x, acc_c)
                acc_l = pick(wz[:, lz - LANES:lz], LANES - 1, 2 * x, acc_l)
            return hy, hz, acc_c, acc_l, acc_g

        zero = jnp.zeros((ly, lz), f32)
        return lax.fori_loop(0, lx, one, (zero, zero, zero1, zero1, zero1), unroll=U_PRE)[2:]

    flags = tuple((me[a] > 0).astype(f32) for a in range(3))

    def pad_high(t):
        return jnp.concatenate([jnp.zeros((ly, lz - LANES), f32), t], 1) if lz > LANES else t

    def halos(phase):
        fx, fy, fz = flags
        for msg in (EX, PX, D1, D2):
            wait_recv(msg, phase)
        d1 = pad_high(pltpu.roll(r_d1[phase], LANES - 1, 1))
        hy_x = (r_px[phase, 0] + half * x_e[phase, 1]) * fx - jnp.where(lane == lz - 1, half * d1, 0.0)
        d2 = jnp.broadcast_to(r_d2[phase, 0:1, :], (ly, lz))
        hz_x = (r_px[phase, 1] - half * x_e[phase, 0]) * fx + jnp.where(row == ly - 1, half * d2, 0.0)
        c0, c1 = c_v[0], c_v[lx - 1]
        dhy = half * r_ex[phase, 1]
        dhz = -half * r_ex[phase, 0]
        h_v[1, lx - 1] = h_v[1, lx - 1] + dhy
        h_v[2, lx - 1] = h_v[2, lx - 1] + dhz
        planes = (
            (1, 0, c0 * hz_x), (2, 0, -c0 * hy_x),
            (0, lx - 1, c1 * ((dhz - down(dhz, 0)) - (dhy - down(dhy, 1)))),
            (1, lx - 1, -c1 * dhz), (2, lx - 1, c1 * dhy),
        )
        for comp, x, d in planes:
            e_v[comp, x] = e_v[comp, x] + d
        for msg in (EZ, PZ, D5, D6):
            wait_recv(msg, phase)
        own = pltpu.roll(z_e[phase], 1, 1)
        low = lane1 < off
        zh = (r_pz[phase] + jnp.where(low, -half * own, half * own)) * fz
        d5 = jnp.broadcast_to(pltpu.roll(r_d5[phase], off, 1)[0:1, :], (ly, LANES))
        zh = zh - jnp.where((row1 == ly - 1) & (lane1 >= off), half * d5, 0.0)
        d6 = pltpu.roll(r_d6[phase], off, 1)
        zh = zh + jnp.where(lane1 == off - 1, half * d6, 0.0)
        ze = half * r_ez[phase]
        odd = lax.rem(lane1, 2) == 1
        cols = jnp.where(odd, jnp.where(low, zh, -zh), ze)
        dhy = jnp.where(odd | (lane1 >= off), 0.0, -ze)
        dhx = jnp.where(odd | (lane1 >= off), 0.0, pltpu.roll(ze, LANES - off, 1))
        shift_x = jnp.where(lane1 < 2, 0.0, pltpu.roll(dhy, 2, 1))
        last = (dhy - shift_x) - (dhx - down(dhx, 0))
        for msg in (EY, PY, D3, D4):
            wait_recv(msg, phase)
        rx = lax.broadcasted_iota(jnp.int32, (lx, LANES), 0)
        cx = lax.broadcasted_iota(jnp.int32, (lx, LANES), 1)
        d4 = jnp.broadcast_to(r_d4[phase, ROWS - 1:ROWS, :], (lx, LANES))
        d4 = jnp.sum(jnp.where(cx == off + 2 * rx, d4, 0.0), axis=1, keepdims=True)
        ry = lax.broadcasted_iota(jnp.int32, (lx, lz), 0)
        cy = lax.broadcasted_iota(jnp.int32, (lx, lz), 1)
        hx_y = (wide(r_py[phase, 0]) - half * wide(y_e[phase, 1])) * fy + jnp.where(cy == lz - 1, half * d4, 0.0)
        d3 = jnp.broadcast_to(r_d3[phase, ROWS - 1:ROWS, :], (lx, lz))
        hz_y = (wide(r_py[phase, 1]) + half * wide(y_e[phase, 0])) * fy - jnp.where(ry == lx - 1, half * d3, 0.0)
        dhx = -half * wide(r_ey[phase, 1])
        dhz = half * wide(r_ey[phase, 0])
        values = (-hz_y, hx_y, dhz, (dhx - down(dhx, 1)) - (dhz - down(dhz, 0)), -dhx)
        for i, v in enumerate(values):
            put_wide(rows_v, i, v)
        return planes, values, cols, last

    cyw = lax.broadcasted_iota(jnp.int32, (lx, lz), 1)

    def first_rows(values, cols, last):
        for x in (0, lx - 1):
            for i, (src, comp, r) in enumerate((
                (e_v, 0, 0), (e_v, 2, 0), (e_v, 0, -1), (e_v, 1, -1), (e_v, 2, -1), (h_v, 0, -1), (h_v, 2, -1))):
                put(y_b, i, x, src[comp, x], r % ly)

        def edge(col, y, at_lane, to):
            t = jnp.where(cx1 == 2 * rx1 + at_lane, jnp.broadcast_to(col[y:y + 1], (lx, LANES)), 0.0)
            return jnp.where(cyw == to, jnp.sum(t, axis=1, keepdims=True), 0.0)

        b = [wide(y_b[i]) for i in range(9)]
        y, end = ly - 1, lz - 1
        hx_edge = edge(cols, y, off, end)
        ex0 = b[0] + b[7] * (values[0] + edge(cols, 0, 1, 0) + edge(cols, 0, 0, end))
        ez0 = b[1] + b[7] * (values[1] + edge(last, 0, 0, end))
        put_wide(y_e.at[1], 0, ex0)
        put_wide(y_e.at[1], 1, ez0)
        ex = b[2] + b[8] * (values[2] + edge(cols, y, 1, 0) + edge(cols, y, 0, end))
        ey = b[3] + b[8] * (values[3] + edge(cols, y, off + 1, 0) + hx_edge)
        ez = b[4] + b[8] * (values[4] + edge(last, y, 0, end))
        top_y(1, ex, ey, ez, b[5] - values[4] + hx_edge, b[6] + values[2])
        d_r[0] = jnp.broadcast_to(ex0[lx - 1:lx], (ROWS, lz))
        d_r[1] = jnp.broadcast_to(ey[0:1], (ROWS, lz))
        lines(1, ey, ez0)

    def gradient_part(planes, values, cols, last, acc_c, acc_l, acc_g):
        w = [wide(y_b[i]) for i in range(5)]
        total = acc_g
        for y, t in ((0, values[0] * w[0] + values[1] * w[1]), (ly - 1, values[2] * w[2] + values[3] * w[3] + values[4] * w[4])):
            t = jnp.sum(t, axis=1, keepdims=True)
            t = jnp.sum(jnp.where(cx1 == 2 * rx1, t, 0.0), axis=0, keepdims=True)
            total = total + jnp.where(row1 == y, t, 0.0)
        p = cols * acc_c
        q = p + pltpu.roll(p, LANES - 1, 1)
        q = q + pltpu.roll(q, LANES - off, 1) + last * acc_l
        total = total + jnp.where((lane1 < off) & (lax.rem(lane1, 2) == 0), q, 0.0)
        for x in (0, lx - 1):
            t = None
            for comp, at_x, d in planes:
                if at_x == x:
                    change = s_v[STEPS - 1, comp, x].astype(f32) - s_v[STEPS, comp, x].astype(f32)
                    t = d * change if t is None else t + d * change
            total = total + jnp.where(lane1 == 2 * x, jnp.sum(t, axis=1, keepdims=True), 0.0)
        return total

    top, bottom = row8 == 0, row8 == ROWS - 1
    lane8 = lax.broadcasted_iota(jnp.int32, (ROWS, LANES), 1)
    first_lane, last_lane = lane8 == 0, lane8 == LANES - 1
    nr = ly // ROWS

    def post(step, cols, last):
        def one(x, acc):
            low_col = pltpu.roll(cols, rem(2 * LANES - (2 * x + 1), LANES), 1)
            high_col = pltpu.roll(cols, rem(2 * LANES - (off + 2 * x + 1), LANES), 1)
            last_col = pltpu.roll(last, rem(2 * LANES - (2 * x + 1), LANES), 1)
            def delta(r, k, col0, col1, row0, row1_):
                terms = []
                cut = slice(r * ROWS, (r + 1) * ROWS)
                if col0 is not None and k == 0:
                    terms.append(jnp.where(first_lane, col0[cut], 0.0))
                if col1 is not None and k == nt - 1:
                    terms.append(jnp.where(last_lane, col1[cut], 0.0))
                if row0 is not None and r == 0:
                    t = jnp.broadcast_to(rows_v[row0, k, pl.ds(x, 1), :], (ROWS, LANES))
                    terms.append(jnp.where(top, t, 0.0))
                if row1_ is not None and r == nr - 1:
                    t = jnp.broadcast_to(rows_v[row1_, k, pl.ds(x, 1), :], (ROWS, LANES))
                    terms.append(jnp.where(bottom, t, 0.0))
                return sum(terms[1:], terms[0]) if terms else None

            new = []
            for comp, args in enumerate(((low_col, low_col, 0, 2), (high_col, high_col, None, 3), (None, last_col, 1, 4))):
                strips = []
                for k in range(nt):
                    strip = []
                    for r in range(nr):
                        at_ = (comp, x, pl.ds(r * ROWS, ROWS), pl.ds(k * LANES, LANES))
                        d = delta(r, k, *args)
                        v = e_v[at_]
                        if d is not None:
                            v = v + c_v[x, r * ROWS:(r + 1) * ROWS, k * LANES:(k + 1) * LANES] * d
                            e_v[at_] = v
                        strip.append(v)
                    strips.append(jnp.concatenate(strip, 0) if nr > 1 else strip[0])
                new.append(strips)
            for comp, args in enumerate((
                ((None, high_col, None, None, 1), (None, None, None, 4, -1)),
                ((None, low_col, None, None, -1),),
                ((None, None, None, 2, 1),),
            )):
                for r in range(nr):
                    for k in range(nt):
                        at_ = (comp, x, pl.ds(r * ROWS, ROWS), pl.ds(k * LANES, LANES))
                        v = None
                        for *which, sign in args:
                            d = delta(r, k, *which)
                            if d is not None:
                                v = h_v[at_] if v is None else v
                                v = v + d if sign > 0 else v - d
                        if v is not None:
                            h_v[at_] = v
            return pick_e(x, wide(new[0]), wide(new[1]), acc) if step + 1 < STEPS else acc

        if step + 1 == STEPS:
            return lax.fori_loop(0, lx, one, zero1, unroll=U_POST)
        acc = lax.fori_loop(0, lx, one, zero1, unroll=U_POST)
        save_e(step + 1)
        for msg in (D1, D6, EX):
            send(msg, step + 1)
        top_x(step + 1, e_v[0, lx - 1], e_v[1, lx - 1], e_v[2, lx - 1], h_v[1, lx - 1], h_v[2, lx - 1])
        send(PX, step + 1)
        return acc

    pl.semaphore_wait(barrier, count)
    for msg in (D2, D3, D1, D6, EX):
        send(msg, 0)

    def first_top(x, carry):
        for i, (src, comp) in enumerate(((e_v, 0), (e_v, 1), (e_v, 2), (h_v, 0), (h_v, 2))):
            put(y_t, i, x, src[comp, x, ly - ROWS:ly, :], ROWS - 1)
        return carry

    def first_pack(x, acc):
        ex, ey = e_v[0, x], e_v[1, x]
        put(y_e.at[0], 0, x, ex, 0)
        put(y_e.at[0], 1, x, e_v[2, x], 0)
        return pick_e(x, ex, ey, acc)

    load_e[0].wait()
    load_h[0].wait()
    lax.fori_loop(0, lx, first_top, 0, unroll=U_PACK)
    top_rows = [wide(y_t[i]) for i in range(5)]
    top_y(0, *top_rows)
    send(PY, 0)
    load_e[1].wait()
    load_m.start()
    load_s.start()
    z_e[0] = lax.fori_loop(0, lx, first_pack, zero1, unroll=U_PACK)
    lines(0, top_rows[1], wide(y_e[0, 1]))
    for msg in (EY, D4, D5, EZ):
        send(msg, 0)
    load_h[1].wait()
    top_x(0, e_v[0, lx - 1], e_v[1, lx - 1], e_v[2, lx - 1], h_v[1, lx - 1], h_v[2, lx - 1])
    send(PX, 0)
    magnetic(0)
    send(PZ, 0)
    save_e(0)

    for c in load_small:
        c.wait()
    plane = extent[1] * extent[2]
    port_x = []
    for p in range(nport):
        cell = ports[p]
        px = lax.div(cell, plane)
        rest = lax.rem(cell, plane)
        py = lax.div(rest, extent[2]) - start[1]
        pz = lax.rem(rest, extent[2]) - start[2]
        port_x.append(px - start[0])
        hit = (row == py) & (lane == pz)
        for s in range(STEPS):
            src_v[s, p] = jnp.where(hit, amps[s, p], 0.0)
    for s in range(STEPS):
        src_v[s, nport] = jnp.zeros((ly, lz), f32)
    coefs = [half / jnp.full((ly, lz), perm[k], f32) for k in range(nmat)]
    load_m.wait()
    pre(0)
    planes, values, cols, last = halos(0)
    first_rows(values, cols, last)
    for msg in (EY, PY, D2, D3, D4, D5):
        send(msg, 1)
    z_e[1] = post(0, cols, last)
    send(EZ, 1)
    magnetic(1)
    send(PZ, 1)
    load_s.wait()
    weights = pre(1)
    spread = lax.broadcasted_iota(jnp.int32, (lx, LANES), 1) == 2 * lax.broadcasted_iota(jnp.int32, (lx, LANES), 0)
    mask = jnp.dot(mask_v[...].astype(f32), spread.astype(f32), preferred_element_type=f32)
    planes, values, cols, last = halos(1)
    acc = gradient_part(planes, values, cols, last, *weights)

    own_rows = ly // nz_dev
    tile = g_out.shape[0]
    g_v[...] = acc * mask

    def tile_of(k):
        return pl.ds(pl.multiple_of((k * own_rows) // tile * tile, ROWS), tile)

    gcopies = []
    for d in range(1, nz_dev):
        peer = lax.rem(me[2] + d, nz_dev)
        gcopies.append(pltpu.make_async_remote_copy(
            src_ref=g_v.at[tile_of(peer)], dst_ref=r_g.at[d - 1],
            send_sem=gs_sem.at[d - 1], recv_sem=gr_sem.at[d - 1],
            device_id=(me[0], me[1], peer), device_id_type=pl.DeviceIdType.MESH))
    for c in gcopies:
        c.start()
    post(1, cols, last)
    for phase in range(STEPS):
        for msg in range(12):
            wait_send(msg, phase)
    total = g_v[tile_of(me[2])]
    for d, c in enumerate(gcopies):
        c.wait_recv()
        total = total + r_g[d]
    shift = lax.rem(tile - lax.rem(me[2] * own_rows, tile), tile)
    g_out[...] = pltpu.roll(total, shift, 0)
    for c in gcopies:
        c.wait_send()


def write_out(e_v, h_v, g_v, e_out, h_out, g_out, sem):
    lx = h_v.shape[1]
    outs = [
        pltpu.make_async_copy(e_v.at[:, 0:lx], e_out, sem.at[0]),
        pltpu.make_async_copy(h_v, h_out, sem.at[1]),
    ]
    for c in outs:
        c.start()
    own, _ = g_out.shape
    pick = lax.broadcasted_iota(jnp.int32, (LANES, LANES), 0) == 2 * lax.broadcasted_iota(jnp.int32, (LANES, LANES), 1)
    g = jnp.dot(g_v[...], pick.astype(jnp.float32), precision=lax.Precision.HIGHEST, preferred_element_type=jnp.float32)
    g_out[...] = g[0:own, 0:lx]
    for c in outs:
        c.wait()


def solution(mesh):
    mesh_sizes = tuple(mesh.shape[a] for a in AXES)

    def body(e_adjoint, h_adjoint, snapshots, material, permittivity, design_mask, ports, amplitudes):
        _, lx, ly, lz = e_adjoint.shape
        extent = (lx * mesh_sizes[0], ly * mesh_sizes[1], lz * mesh_sizes[2])
        nport = ports.shape[0]
        nt = lz // LANES
        f32 = jnp.float32
        own = ly // mesh_sizes[2]
        tile = max(ROWS, own)
        any_spec = pl.BlockSpec(memory_space=pl.ANY)
        vmem = pl.BlockSpec(memory_space=pltpu.VMEM)
        e, h, g = pl.pallas_call(
            lambda *refs: kernel(mesh_sizes, extent, *refs),
            out_shape=(
                pltpu.VMEM((3, lx + 1, ly, lz), f32),
                pltpu.VMEM((3, lx, ly, lz), f32),
                pltpu.VMEM((tile, LANES), f32),
            ),
            in_specs=[any_spec, any_spec, any_spec, any_spec, any_spec, any_spec, any_spec, any_spec],
            out_specs=(vmem, vmem, vmem),
            scratch_shapes=[
                pltpu.VMEM(snapshots.shape, snapshots.dtype),
                pltpu.VMEM((lx, ly, lz), jnp.int32),
                pltpu.VMEM((lx, ly, lz), f32),
                pltpu.VMEM((STEPS, nport + 1, ly, lz), f32),
                pltpu.VMEM((STEPS, 3, ly, lz), f32),
                pltpu.VMEM((STEPS, 2, nt, lx, LANES), f32),
                pltpu.VMEM((STEPS, ly, LANES), f32),
                pltpu.VMEM((STEPS, 2, ly, lz), f32),
                pltpu.VMEM((STEPS, 2, nt, lx, LANES), f32),
                pltpu.VMEM((STEPS, ly, LANES), f32),
                pltpu.VMEM((5, nt, lx, LANES), f32),
                pltpu.VMEM((9, nt, lx, LANES), f32),
                pltpu.VMEM((2, ROWS, lz), f32),
                pltpu.VMEM((STEPS, 2, ROWS, LANES), f32),
                pltpu.VMEM((5, nt, lx, LANES), f32),
                pltpu.VMEM((ly, LANES), f32),
                pltpu.VMEM((STEPS, 2, ly, lz), f32),
                pltpu.VMEM((STEPS, 2, nt, lx, LANES), f32),
                pltpu.VMEM((STEPS, ly, LANES), f32),
                pltpu.VMEM((STEPS, 2, ly, lz), f32),
                pltpu.VMEM((STEPS, 2, nt, lx, LANES), f32),
                pltpu.VMEM((STEPS, ly, LANES), f32),
                pltpu.VMEM((STEPS, ly, LANES), f32),
                pltpu.VMEM((STEPS, ROWS, lz), f32),
                pltpu.VMEM((STEPS, ROWS, lz), f32),
                pltpu.VMEM((STEPS, ROWS, LANES), f32),
                pltpu.VMEM((STEPS, ROWS, LANES), f32),
                pltpu.VMEM((STEPS, ly, LANES), f32),
                pltpu.VMEM((3, tile, LANES), f32),
                pltpu.SMEM(permittivity.shape, f32),
                pltpu.SMEM(ports.shape, jnp.int32),
                pltpu.SMEM(amplitudes.shape, f32),
                pltpu.VMEM((ly, lx), jnp.int32),
                pltpu.SemaphoreType.DMA((10,)),
                pltpu.SemaphoreType.DMA((STEPS, 12)),
                pltpu.SemaphoreType.DMA((STEPS, 12)),
                pltpu.SemaphoreType.DMA((3,)),
                pltpu.SemaphoreType.DMA((3,)),
            ],
            compiler_params=pltpu.CompilerParams(collective_id=0, has_side_effects=True),
            name="reverse_steps",
        )(permittivity, ports, amplitudes, design_mask.T, e_adjoint, h_adjoint, snapshots, material)
        e, h, g = (pltpu.with_memory_space_constraint(v, pltpu.VMEM) for v in (e, h, g))
        e, h, g = pl.pallas_call(
            write_out,
            out_shape=(
                jax.ShapeDtypeStruct(e_adjoint.shape, f32),
                jax.ShapeDtypeStruct(h_adjoint.shape, f32),
                jax.ShapeDtypeStruct((own, lx), f32),
            ),
            in_specs=[vmem, vmem, vmem],
            out_specs=(any_spec, any_spec, vmem),
            scratch_shapes=[pltpu.SemaphoreType.DMA((2,))],
            name="write_out",
        )(e, h, g)
        return e, h, g.T

    placed = (
        P(None, "gx", "gy", "gz"),
        P(None, "gx", "gy", "gz"),
        P(None, None, "gx", "gy", "gz"),
        P("gx", "gy", "gz"),
        P(),
        P("gx", "gy"),
        P(),
        P(),
    )
    return jax.shard_map(
        body,
        mesh=mesh,
        in_specs=placed,
        out_specs=(P(None, "gx", "gy", "gz"), P(None, "gx", "gy", "gz"), P("gx", ("gy", "gz"))),
        check_vma=False,
    )
```
